128 devices in a mesh: aux: 8 (over x, core), basis: 16 (over z, y).
Axes of the slice: x: 4, y: 4, z: 4, core: 2. Of those that a mesh axis runs over, the one named last changes fastest.
Arguments:
- v_blocks: bfloat16 [64, 768, 128, 128], P('aux', 'basis'), may hold values from -6 to 6
- pair_map: int32 [8, 768, 2], P('aux', 'basis'), may hold values from 0 to 239, as said below
- pair_count: int32 [8, 16], P('aux', 'basis'), may hold values from 2 to 48, as said below
- occ_coef: bfloat16 [8, 30720], P(None, 'basis'), may hold values from -0.375 to 0.375
- virt_coef: bfloat16 [30720, 32768], P('basis', 'aux'), may hold values from -0.03125 to 0.03125
Outputs:
- b_tensor: bfloat16 [32768, 512], P(('aux', 'basis'))
The draws below stay inside these ranges and needn't reach their ends.
Inputs may be any that keep to these rules, and one draw needn't show every extreme that they name: pair_map[s, k, 0] lies in the blocks of basis index k // 48 (blocks b * 240 / 16 onward); pair_map[s, k, 1] lies within 8 blocks of it, cyclically over 240 blocks, and that distance 8 is reached. Only the first pair_count slots of a device are live; in every slab some basis index has all 48 live.
All inputs are finite; a program needn't handle non-finite values.
Results may differ from the reference program's by a relative error of at most 0.0049.
Values may be sent and summed in bfloat16 or wider, within the bound.
A program may use at most 192 MiB of HBM per device.

```python
import jax
import jax.numpy as jnp
from jax import lax

NBF = 30720
BB = 128
NVIR = 32768
NOCC = 8
NEAR = 8
P_DEV = 8
PAIR_CAP = 48
NB = 240
NAUXW = 64
PAIRS = 768
N_AUX = 8
N_BASIS = 16


def draw_pair_count(key, part):
    key_centre, key_jitter = jax.random.split(jax.random.fold_in(key, 11))
    centre = jax.random.randint(key_centre, (N_AUX, 1), 0, N_BASIS)
    devices = jnp.arange(N_BASIS)[None, :]
    distance = jnp.abs(devices - centre)
    distance = jnp.minimum(distance, N_BASIS - distance)
    base_count = PAIR_CAP * 4 // (4 + distance)
    jitter = jax.random.randint(key_jitter, (N_AUX, N_BASIS), 0, 3)
    counts = jnp.where(distance == 0, PAIR_CAP, jnp.maximum(base_count - jitter, 2))
    return counts.astype(jnp.int32)


def draw_pair_map(key, part):
    key_mu, key_nu = jax.random.split(jax.random.fold_in(key, 23))
    blocks_here = NB // N_BASIS
    local_block = jax.random.randint(key_mu, (N_AUX, N_BASIS, PAIR_CAP), 0, blocks_here)
    mu_block = local_block + jnp.arange(N_BASIS)[None, :, None] * blocks_here
    offsets = jax.random.randint(key_nu, (N_AUX, N_BASIS, PAIR_CAP), -NEAR, NEAR + 1)
    slot_index = jnp.arange(PAIR_CAP)[None, None, :]
    offsets = jnp.where(slot_index == 0, NEAR, jnp.where(slot_index == 1, -NEAR, offsets))
    nu_block = jnp.mod(mu_block + offsets, NB)
    stacked = jnp.stack([mu_block, nu_block], axis=-1)
    return stacked.reshape(N_AUX, N_BASIS * PAIR_CAP, 2).astype(jnp.int32)


def block_scale(stream_key, shape, pieces, low, high):
    def one(position, shards_of):
        steps = jax.random.uniform(jax.random.fold_in(jax.random.fold_in(stream_key, 6), position), (shards_of,), jnp.float32, low / len(pieces), high / len(pieces))
        return jnp.repeat(jnp.exp(steps), shape[position] // shards_of).reshape((-1,) + (1,) * (len(shape) - position - 1))

    level = one(*pieces[0])
    for cut in pieces[1:]:
        level = level * one(*cut)
    return level


def centred(stream_key, shape, scale, reach, cuts=(), dtype=jnp.bfloat16):
    drawn = scale * jax.random.normal(stream_key, shape, jnp.float32)
    if cuts:
        drawn = drawn * block_scale(stream_key, shape, cuts, -0.22, 0.18)
    return jnp.clip(drawn, -reach, reach).astype(dtype)


def setup_inputs(seed: int = 0) -> dict:
    key_list = jax.random.split(jax.random.key(seed), 6)
    v_blocks = centred(key_list[0], (NAUXW, PAIRS, BB, BB), 1.0, 6.0, ((0, 8), (1, 16)))
    pair_map = draw_pair_map(jax.random.fold_in(key_list[5], 71), 0)
    pair_count = draw_pair_count(jax.random.fold_in(key_list[5], 71), 0)
    occ_coef = centred(key_list[3], (NOCC, NBF), (2 * BB) ** -0.5, 0.375, ((1, 16),))
    virt_coef = centred(key_list[4], (NBF, NVIR), NBF ** -0.5, 0.03125, ((0, 16), (1, 8)))
    return dict(v_blocks=v_blocks, pair_map=pair_map, pair_count=pair_count, occ_coef=occ_coef, virt_coef=virt_coef)


def reference(v_blocks, pair_map, pair_count, occ_coef, virt_coef):
    occ_table = occ_coef.astype(jnp.float32).reshape(NOCC, NB, BB)
    slot_index = jnp.arange(N_BASIS * PAIR_CAP).astype(jnp.int32)
    slab_list = []
    for slab in range(N_AUX):
        mu_block = pair_map[slab, :, 0]
        nu_block = pair_map[slab, :, 1]
        live_slots = ((slot_index % PAIR_CAP) < pair_count[slab, slot_index // PAIR_CAP]).astype(jnp.float32)
        picked = jnp.take(occ_table, nu_block, axis=1)
        slab_blocks = v_blocks[slab * P_DEV:(slab + 1) * P_DEV].astype(jnp.float32)
        half_sums = jnp.einsum("qkmn,ikn->qikm", slab_blocks, picked, precision=lax.Precision.HIGHEST)
        half_sums = half_sums * live_slots[None, None, :, None]
        owner_map = (mu_block[:, None] == jnp.arange(NB).astype(jnp.int32)[None, :]).astype(jnp.float32)
        local_half = jnp.einsum("qikm,kb->qibm", half_sums, owner_map, precision=lax.Precision.HIGHEST)
        slab_list.append(local_half.reshape(P_DEV * NOCC, NBF).astype(jnp.bfloat16))
    half_rows = jnp.concatenate(slab_list, axis=0)
    result = lax.dot_general(virt_coef, half_rows, (((0,), (1,)), ((), ())), preferred_element_type=jnp.float32)
    return result.astype(jnp.bfloat16)
```

```python
import functools

import jax
import jax.numpy as jnp
from jax import lax
from jax.experimental import pallas as pl
from jax.experimental.pallas import tpu as pltpu
from jax.sharding import PartitionSpec as P

BB = 128
NOCC = 8
NEAR = 8
PAIR_CAP = 48
NB = 240
Q = 8
HERE = 15
ROWS = HERE * BB
COLS = 4096
TILE = 256
SIDE = 4
PIECES = 4
GROUPS = ((0, 128), (128, 256), (384, 128))
MESH = pl.DeviceIdType.MESH
F32 = jnp.float32
BF16 = jnp.bfloat16


def kernel(
    pm,
    pc,
    v_hbm,
    occ_hbm,
    virt_hbm,
    out_ref,
    v,
    virt,
    occ,
    halo,
    tab,
    lhs,
    hall,
    part,
    rel1,
    in1,
    tsum,
    own,
    rel2,
    in2,
    vsem,
    wsem,
    osem,
    hs,
    hr,
    gs,
    gr,
    ss,
    sr,
):
    aux = lax.axis_index("aux")
    basis = lax.axis_index("basis")
    x, c = aux // 2, aux % 2
    z, y = basis // SIDE, basis % SIDE

    partner = (2 * x + 1 - c, basis)
    x_up = (2 * ((x + 1) % SIDE) + c, basis)
    x_down = (2 * ((x + 3) % SIDE) + c, basis)
    y_up = (aux, z * SIDE + (y + 1) % SIDE)
    y_down = (aux, z * SIDE + (y + 3) % SIDE)
    z_up = (aux, ((z + 1) % SIDE) * SIDE + y)
    z_down = (aux, ((z + 3) % SIDE) * SIDE + y)
    b_up = (aux, (basis + 1) % (SIDE * SIDE))
    b_down = (aux, (basis + SIDE * SIDE - 1) % (SIDE * SIDE))

    def remote(src, dst, send, recv, peer):
        return pltpu.make_async_remote_copy(
            src_ref=src,
            dst_ref=dst,
            send_sem=send,
            recv_sem=recv,
            device_id={"aux": peer[0], "basis": peer[1]},
            device_id_type=MESH,
        )

    v_copies = [
        pltpu.make_async_copy(v_hbm.at[pl.ds(2 * p, 2)], v.at[pl.ds(2 * p, 2)], vsem.at[p])
        for p in range(PIECES)
    ]
    occ_copy = pltpu.make_async_copy(occ_hbm, occ, osem)
    occ_copy.start()
    for copy in v_copies:
        copy.start()

    barrier = pltpu.get_barrier_semaphore()
    peers = (partner, x_up, x_down, y_up, y_down, z_up, z_down, b_up, b_down)
    for peer in peers:
        pl.semaphore_signal(
            barrier, inc=1, device_id={"aux": peer[0], "basis": peer[1]}, device_id_type=MESH
        )
    pl.semaphore_wait(barrier, len(peers))

    started = []

    def go(copy):
        copy.start()
        started.append(copy)

    width = NEAR * BB
    to_up = remote(occ_hbm.at[:, pl.ds(ROWS - width, width)], halo.at[0], hs.at[0], hr.at[0], b_up)
    to_down = remote(occ_hbm.at[:, pl.ds(0, width)], halo.at[1], hs.at[1], hr.at[1], b_down)
    go(to_up)
    go(to_down)
    virt_copies = [
        pltpu.make_async_copy(
            virt_hbm.at[:, pl.ds(j * 1024, 1024)], virt.at[:, pl.ds(j * 1024, 1024)], wsem.at[j]
        )
        for j in range(SIDE)
    ]
    occ_copy.wait()
    for j in range(HERE):
        tab[NEAR + j] = occ[:, j * BB : (j + 1) * BB].astype(F32)
    to_up.wait_recv()
    to_down.wait_recv()
    for copy in virt_copies:
        copy.start()
    for j in range(NEAR):
        tab[j] = halo[0, :, j * BB : (j + 1) * BB].astype(F32)
        tab[NEAR + HERE + j] = halo[1, :, j * BB : (j + 1) * BB].astype(F32)

    first = basis * HERE
    row_block = lax.broadcasted_iota(jnp.int32, (BB, BB), 0) // NOCC

    def build(k, _):
        mu = pm[0, k, 0]
        nu = pm[0, k, 1]
        place = jnp.where(k < pc[0, 0], mu - first, -1)
        pos = jnp.clip(lax.rem(nu - first + NEAR + NB, NB), 0, HERE + 2 * NEAR - 1)
        picked = tab[pos]
        stack = jnp.concatenate([picked] * (BB // NOCC), axis=0)
        lhs[:, pl.ds(pl.multiple_of(k * BB, BB), BB)] = jnp.where(
            row_block == place, stack, 0.0
        ).astype(BF16)
        return 0

    lax.fori_loop(0, PAIR_CAP, build, 0)

    def piece_row(position, core, p):
        return pl.multiple_of(position * 128 + core * 64 + p * 16, 16)

    def rows16(row):
        return hall.at[pl.ds(row, 16)]

    def gather(message, p, position_src, position_dst, core, peer):
        return remote(
            rows16(piece_row(position_src, core, p)),
            rows16(piece_row(position_dst, core, p)),
            gs.at[message, p],
            gr.at[message, p],
            peer,
        )

    def arrived(message, p, position, core, peer):
        ref = rows16(piece_row(position, core, p))
        remote(ref, ref, gs.at[message, p], gr.at[message, p], peer).wait_recv()

    for p in range(PIECES):
        v_copies[p].wait()
        acc = jnp.zeros((BB, 2 * BB), F32)
        for k in range(0, PAIR_CAP, 2):
            w = jnp.concatenate(
                [
                    jnp.concatenate([v[2 * p + e, k], v[2 * p + e, k + 1]], axis=1)
                    for e in range(2)
                ],
                axis=0,
            )
            acc += lax.dot_general(
                lhs[:, k * BB : (k + 2) * BB],
                w,
                (((1,), (1,)), ((), ())),
                preferred_element_type=F32,
            )
        row = piece_row(0, c, p)
        for j in range(HERE):
            lines = acc[j * NOCC : (j + 1) * NOCC]
            both = jnp.concatenate([lines[:, :BB], lines[:, BB:]], axis=0)
            hall[pl.ds(row, 16), j * BB : (j + 1) * BB] = both.astype(BF16)
        go(gather(0, p, 0, 0, c, partner))
        go(gather(1, p, 0, 2, c, x_up))
        go(gather(2, p, 0, 1, c, x_down))

    relay_peer = (2 * ((x + 1 + 2 * c) % SIDE) + c, basis)

    def forward_near():
        for p in range(PIECES):
            arrived(1, p, 2, c, x_down)
            go(gather(3, p, 2, 2, c, partner))
            arrived(2, p, 1, c, x_up)
            go(gather(4, p, 1, 1, c, partner))
            go(gather(5, p, 2 - c, 3, c, relay_peer))

    def forward_far():
        for p in range(PIECES):
            arrived(5, p, 3, c, relay_peer)
            go(gather(6, p, 3, 3, c, partner))

    def chunk(g, zt, yt):
        r0, rows = GROUPS[g]
        column = pl.multiple_of((zt * SIDE + yt) * TILE, TILE)
        acc = jnp.dot(
            hall[pl.ds(r0, rows), :], virt[:, pl.ds(column, TILE)], preferred_element_type=F32
        )
        part[zt, yt, pl.ds(r0, rows), :] = acc.astype(BF16)

    def at(here, delta):
        return (here + delta) % SIDE

    def segment(g, fixed, delta, count, start):
        def body(i, _):
            other = i + start
            if fixed == "y":
                chunk(g, at(z, other), at(y, delta))
            else:
                chunk(g, at(z, delta), at(y, other))
            return 0

        lax.fori_loop(0, count, body, 0)

    def lines(g, half, which):
        r0, rows = GROUPS[g]
        quarter = rows // 4
        return (
            pl.ds(r0 + half * 2 * quarter + which * quarter, quarter),
            pl.ds(r0 // 2 + which * quarter, quarter),
            pl.ds(r0 // 4, quarter),
        )

    def ring(half, phase):
        along_y = half == phase
        return (y, y_up, y_down) if along_y else (z, z_up, z_down)

    def messages(g, half, phase):
        here, up, down = ring(half, phase)

        def source(target, which):
            hall_rows, half_rows, _ = lines(g, half, which)
            if phase == 1:
                return tsum.at[half, target, half_rows, :]
            if half == 0:
                return part.at[:, target, hall_rows, :]
            return part.at[target, :, hall_rows, :]

        def relay(direction):
            rows = lines(g, half, 0)[2]
            if phase == 1:
                return rel2.at[half, direction, rows, :]
            return rel1.at[half, direction, :, rows, :]

        def landing(direction, which):
            rows = lines(g, half, which)[1]
            if phase == 1:
                return in2.at[half, direction, rows, :]
            return in1.at[half, direction, :, rows, :]

        def make(j, src, dst, peer):
            return remote(src, dst, ss.at[g, half, phase, j], sr.at[g, half, phase, j], peer)

        return (
            make(0, source(at(here, 2), 0), relay(0), up),
            make(1, source(at(here, 2), 1), relay(1), down),
            make(2, source(at(here, 1), 1), landing(0, 1), up),
            make(3, source(at(here, 1), 0), landing(0, 0), up),
            make(4, source(at(here, 3), 0), landing(1, 0), down),
            make(5, source(at(here, 3), 1), landing(1, 1), down),
        )

    everything = {
        (g, half, phase): messages(g, half, phase)
        for g in range(len(GROUPS))
        for half in range(2)
        for phase in range(2)
    }

    def send(g, half, phase, *which):
        for j in which:
            go(everything[g, half, phase][j])

    def wait(g, half, phase, *which):
        for j in which:
            everything[g, half, phase][j].wait_recv()

    def relay1(g, half):
        here = ring(half, 0)[0]
        for direction, arrival, onward, delta, which in ((0, 0, 3, 1, 0), (1, 1, 5, 3, 1)):
            wait(g, half, 0, arrival)
            hall_rows, _, quarter = lines(g, half, which)
            target = at(here, delta)

            def body(t, _):
                zt, yt = (t, target) if half == 0 else (target, t)
                total = part[zt, yt, hall_rows, :].astype(F32) + rel1[
                    half, direction, t, quarter, :
                ].astype(F32)
                part[zt, yt, hall_rows, :] = total.astype(BF16)
                return 0

            lax.fori_loop(0, SIDE, body, 0)
            send(g, half, 0, onward)

    def middle(g, half):
        wait(g, half, 0, 2, 3, 4, 5)
        r0, rows = GROUPS[g]
        count = rows // 2
        hall_rows = pl.ds(r0 + half * count, count)
        half_rows = pl.ds(r0 // 2, count)
        other = z if half == 0 else y

        def total(delta):
            t = at(other, delta)
            zt, yt = (t, y) if half == 0 else (z, t)
            return t, (
                part[zt, yt, hall_rows, :].astype(F32)
                + in1[half, 0, t, half_rows, :].astype(F32)
                + in1[half, 1, t, half_rows, :].astype(F32)
            )

        for delta, sends in ((2, (0, 1)), (1, (2,)), (3, (4,))):
            t, value = total(delta)
            tsum[half, t, half_rows, :] = value.astype(BF16)
            send(g, half, 1, *sends)
        own[half, half_rows, :] = total(0)[1]

    def relay2(g, half):
        other = z if half == 0 else y
        for direction, arrival, onward, delta, which in ((0, 0, 3, 1, 0), (1, 1, 5, 3, 1)):
            wait(g, half, 1, arrival)
            _, half_rows, quarter = lines(g, half, which)
            target = at(other, delta)
            value = tsum[half, target, half_rows, :].astype(F32) + rel2[
                half, direction, quarter, :
            ].astype(F32)
            tsum[half, target, half_rows, :] = value.astype(BF16)
            send(g, half, 1, onward)

    def finish(g):
        r0, rows = GROUPS[g]
        count = rows // 2
        half_rows = pl.ds(r0 // 2, count)
        totals = []
        for half in range(2):
            wait(g, half, 1, 2, 3, 4, 5)
            totals.append(
                own[half, half_rows, :]
                + in2[half, 0, half_rows, :].astype(F32)
                + in2[half, 1, half_rows, :].astype(F32)
            )
        value = jnp.concatenate(totals, axis=0)
        for position in range(r0 // 128, (r0 + rows) // 128):
            chip = (x + (0, 1, 3, 2)[position]) % SIDE
            block = value[position * 128 - r0 : position * 128 - r0 + 128]
            out_ref[:, pl.ds(pl.multiple_of(chip * 128, 128), 128)] = block.T.astype(BF16)

    def compute(g, between):
        segment(g, "y", 2, 4, 2)
        send(g, 0, 0, 0, 1)
        segment(g, "z", 2, 3, 3)
        send(g, 1, 0, 0, 1)
        between()
        segment(g, "y", 1, 3, 3)
        send(g, 0, 0, 2)
        segment(g, "y", 3, 3, 3)
        send(g, 0, 0, 4)
        segment(g, "y", 0, 3, 3)
        send(g, 1, 0, 2, 4)
        for half in range(2):
            relay1(g, half)

    for p in range(PIECES):
        arrived(0, p, 0, 1 - c, partner)
    for copy in virt_copies:
        copy.wait()

    compute(0, forward_near)

    for p in range(PIECES):
        arrived(3, p, 2, 1 - c, partner)
        arrived(4, p, 1, 1 - c, partner)

    def between1():
        forward_far()
        middle(0, 0)
        middle(0, 1)

    compute(1, between1)
    relay2(0, 0)
    relay2(0, 1)
    for p in range(PIECES):
        arrived(6, p, 3, 1 - c, partner)

    def between2():
        middle(1, 0)
        middle(1, 1)

    compute(2, between2)
    relay2(1, 0)
    relay2(1, 1)
    finish(0)
    middle(2, 0)
    middle(2, 1)
    finish(1)
    relay2(2, 0)
    relay2(2, 1)
    finish(2)
    for copy in started:
        copy.wait_send()


def local(v_blocks, pair_map, pair_count, occ_coef, virt_coef):
    anywhere = pl.BlockSpec(memory_space=pl.ANY)
    scalars = pl.BlockSpec(memory_space=pltpu.SMEM)
    groups = len(GROUPS)
    return pl.pallas_call(
        kernel,
        out_shape=jax.ShapeDtypeStruct((TILE, 512), BF16),
        in_specs=[scalars, scalars, anywhere, anywhere, anywhere],
        out_specs=pl.BlockSpec(memory_space=pltpu.VMEM),
        scratch_shapes=[
            pltpu.VMEM((Q, PAIR_CAP, BB, BB), BF16),
            pltpu.VMEM((ROWS, COLS), BF16),
            pltpu.VMEM((NOCC, ROWS), BF16),
            pltpu.VMEM((2, NOCC, NEAR * BB), BF16),
            pltpu.VMEM((HERE + 2 * NEAR, NOCC, BB), F32),
            pltpu.VMEM((BB, PAIR_CAP * BB), BF16),
            pltpu.VMEM((512, ROWS), BF16),
            pltpu.VMEM((SIDE, SIDE, 512, TILE), BF16),
            pltpu.VMEM((2, 2, SIDE, 128, TILE), BF16),
            pltpu.VMEM((2, 2, SIDE, 256, TILE), BF16),
            pltpu.VMEM((2, SIDE, 256, TILE), BF16),
            pltpu.VMEM((2, 256, TILE), F32),
            pltpu.VMEM((2, 2, 128, TILE), BF16),
            pltpu.VMEM((2, 2, 256, TILE), BF16),
            pltpu.SemaphoreType.DMA((PIECES,)),
            pltpu.SemaphoreType.DMA((SIDE,)),
            pltpu.SemaphoreType.DMA,
            pltpu.SemaphoreType.DMA((2,)),
            pltpu.SemaphoreType.DMA((2,)),
            pltpu.SemaphoreType.DMA((7, PIECES)),
            pltpu.SemaphoreType.DMA((7, PIECES)),
            pltpu.SemaphoreType.DMA((groups, 2, 2, 6)),
            pltpu.SemaphoreType.DMA((groups, 2, 2, 6)),
        ],
        compiler_params=pltpu.CompilerParams(
            collective_id=0, has_side_effects=True, vmem_limit_bytes=60 << 20
        ),
        name="occupied_batch",
    )(pair_map, pair_count, v_blocks, occ_coef, virt_coef)


def solution(mesh):
    in_specs = (
        P("aux", "basis", None, None),
        P("aux", "basis", None),
        P("aux", "basis"),
        P(None, "basis"),
        P("basis", "aux"),
    )
    out_specs = P(("aux", "basis"), None)
    return jax.shard_map(local, mesh=mesh, in_specs=in_specs, out_specs=out_specs, check_vma=False)
```

```python
import functools

import jax
import jax.numpy as jnp
from jax import lax
from jax.experimental import pallas as pl
from jax.experimental.pallas import tpu as pltpu
from jax.sharding import PartitionSpec as P

BB = 128
NOCC = 8
NEAR = 8
PAIR_CAP = 48
NB = 240
Q = 8
HERE = 15
ROWS = HERE * BB
COLS = 4096
TILE = 256
SIDE = 4
PIECES = 4
GROUPS = ((0, 128), (128, 384))
ORDER = (
    (2, 2), (1, 2), (2, 1), (3, 2), (2, 3), (0, 2), (2, 0), (1, 1),
    (3, 1), (1, 3), (3, 3), (0, 1), (1, 0), (0, 3), (3, 0), (0, 0),
)
MESH = pl.DeviceIdType.MESH
F32 = jnp.float32
BF16 = jnp.bfloat16


def kernel(
    pm_hbm,
    pc_hbm,
    v_hbm,
    occ_hbm,
    virt_hbm,
    out_ref,
    pm,
    pc,
    v,
    virt,
    occ,
    halo,
    tab,
    lhs,
    hall,
    part,
    rel1,
    in1,
    tsum,
    own,
    rel2,
    in2,
    isem,
    vsem,
    wsem,
    sends,
    hr,
    gr,
    gr_all,
    r1,
    l1,
    r2,
    l2,
):
    aux = lax.axis_index("aux")
    basis = lax.axis_index("basis")
    x, c = aux // 2, aux % 2
    z, y = basis // SIDE, basis % SIDE

    partner = (2 * x + 1 - c, basis)
    x_up = (2 * ((x + 1) % SIDE) + c, basis)
    x_down = (2 * ((x + 3) % SIDE) + c, basis)
    y_up = (aux, z * SIDE + (y + 1) % SIDE)
    y_down = (aux, z * SIDE + (y + 3) % SIDE)
    z_up = (aux, ((z + 1) % SIDE) * SIDE + y)
    z_down = (aux, ((z + 3) % SIDE) * SIDE + y)
    b_up = (aux, (basis + 1) % (SIDE * SIDE))
    b_down = (aux, (basis + SIDE * SIDE - 1) % (SIDE * SIDE))
    x_relay = (2 * ((x + 1 + 2 * c) % SIDE) + c, basis)

    barrier = pltpu.get_barrier_semaphore()
    peers = (b_up, b_down, z_up, z_down, y_up, y_down, x_up, x_down, partner)
    for peer in peers:
        pl.semaphore_signal(
            barrier, inc=1, device_id={"aux": peer[0], "basis": peer[1]}, device_id_type=MESH
        )

    def remote(src, dst, send, recv, peer):
        return pltpu.make_async_remote_copy(
            src_ref=src,
            dst_ref=dst,
            send_sem=send,
            recv_sem=recv,
            device_id={"aux": peer[0], "basis": peer[1]},
            device_id_type=MESH,
        )

    small = (
        pltpu.make_async_copy(occ_hbm, occ, isem.at[0]),
        pltpu.make_async_copy(pm_hbm, pm, isem.at[1]),
        pltpu.make_async_copy(pc_hbm, pc, isem.at[2]),
    )
    for copy in small:
        copy.start()

    def v_copy(p):
        return pltpu.make_async_copy(v_hbm.at[pl.ds(2 * p, 2)], v.at[pl.ds(2 * p, 2)], vsem.at[p])

    for p in range(PIECES):
        v_copy(p).start()
    virt_copies = [
        pltpu.make_async_copy(
            virt_hbm.at[:, pl.ds(j * 1024, 1024)], virt.at[:, pl.ds(j * 1024, 1024)], wsem.at[j]
        )
        for j in range(SIDE)
    ]
    with jax.named_scope("t_barrier"):
        pl.semaphore_wait(barrier, len(peers))

    width = NEAR * BB
    small[0].wait()
    to_up = remote(occ.at[:, pl.ds(ROWS - width, width)], halo.at[0], sends.at[0], hr.at[0], b_up)
    to_down = remote(occ.at[:, pl.ds(0, width)], halo.at[1], sends.at[0], hr.at[1], b_down)
    to_up.start()
    to_down.start()
    for j in range(HERE):
        tab[NEAR + j] = occ[:, j * BB : (j + 1) * BB].astype(F32)
    small[1].wait()
    small[2].wait()
    with jax.named_scope("t_halo"):
        to_up.wait_recv()
        to_down.wait_recv()
    for copy in virt_copies:
        copy.start()
    for j in range(NEAR):
        tab[j] = halo[0, :, j * BB : (j + 1) * BB].astype(F32)
        tab[NEAR + HERE + j] = halo[1, :, j * BB : (j + 1) * BB].astype(F32)

    first = basis * HERE
    row_block = lax.broadcasted_iota(jnp.int32, (BB, BB), 0) // NOCC

    def build(k, _):
        mu = pm[0, 0, k]
        nu = pm[0, 1, k]
        place = jnp.where(k < pc[0, 0], mu - first, -1)
        pos = jnp.clip(lax.rem(nu - first + NEAR + NB, NB), 0, HERE + 2 * NEAR - 1)
        stack = jnp.concatenate([tab[pos]] * (BB // NOCC), axis=0)
        lhs[:, pl.ds(pl.multiple_of(k * BB, BB), BB)] = jnp.where(
            row_block == place, stack, 0.0
        ).astype(BF16)
        return 0

    with jax.named_scope("t_build"):
        lax.fori_loop(0, PAIR_CAP, build, 0, unroll=4)

    def piece_ref(position, core, p):
        return hall.at[pl.ds(pl.multiple_of(position * 128 + core * 64 + p * 16, 16), 16)]

    def gather_sem(message, p):
        if message in (1, 2, 5):
            return gr.at[(1, 2, 5).index(message), p]
        return gr_all.at[(0, 3, 4, 6).index(message)]

    def gather(message, p, position_src, position_dst, core, peer):
        return remote(
            piece_ref(position_src, core, p),
            piece_ref(position_dst, core, p),
            sends.at[1],
            gather_sem(message, p),
            peer,
        )

    def arrived(message, p, position, core, peer):
        ref = piece_ref(position, core, p)
        remote(ref, ref, sends.at[1], gather_sem(message, p), peer).wait_recv()

    def all_arrived(message, position):
        ref = hall.at[pl.ds(pl.multiple_of(position * 128 + (1 - c) * 64, 64), 64)]
        remote(ref, ref, sends.at[1], gather_sem(message, 0), partner).wait_recv()

    def first_half(p, _):
        v_copy(p).wait()
        acc = jnp.zeros((BB, 2 * BB), F32)
        for k in range(0, PAIR_CAP, 2):
            w = jnp.concatenate(
                [
                    jnp.concatenate([v[2 * p + e, k], v[2 * p + e, k + 1]], axis=1)
                    for e in range(2)
                ],
                axis=0,
            )
            acc += lax.dot_general(
                lhs[:, k * BB : (k + 2) * BB],
                w,
                (((1,), (1,)), ((), ())),
                preferred_element_type=F32,
            )
        row = pl.multiple_of(c * 64 + p * 16, 16)
        for j in range(HERE):
            lines = acc[j * NOCC : (j + 1) * NOCC]
            both = jnp.concatenate([lines[:, :BB], lines[:, BB:]], axis=0)
            hall[pl.ds(row, 16), j * BB : (j + 1) * BB] = both.astype(BF16)
        gather(0, p, 0, 0, c, partner).start()
        gather(1, p, 0, 2, c, x_up).start()
        gather(2, p, 0, 1, c, x_down).start()
        return 0

    with jax.named_scope("t_first"):
        lax.fori_loop(0, PIECES, first_half, 0)

    def forward_near(p, _):
        arrived(1, p, 2, c, x_down)
        gather(3, p, 2, 2, c, partner).start()
        arrived(2, p, 1, c, x_up)
        gather(4, p, 1, 1, c, partner).start()
        gather(5, p, 2 - c, 3, c, x_relay).start()
        return 0

    def forward_far(p, _):
        arrived(5, p, 3, c, x_relay)
        gather(6, p, 3, 3, c, partner).start()
        return 0

    def rows_of(g, half, which, count=1):
        r0, rows = GROUPS[g]
        quarter = rows // 4
        return (
            r0 + half * 2 * quarter + which * quarter,
            r0 // 2 + which * quarter,
            r0 // 4,
            quarter * count,
        )

    def ring(half, phase):
        return (y, y_up, y_down) if half == phase else (z, z_up, z_down)

    KINDS = ((0, 0, 0), (1, 1, 0), (1, 0, 1), (0, 0, 1), (0, 1, 1), (1, 1, 1))

    def message1(g, half, j, target, t):
        which, way, landing = KINDS[j]
        hall_row, half_row, quarter_row, n = rows_of(g, half, which)
        zt, yt = (t, target) if half == 0 else (target, t)
        if landing:
            dst = in1.at[half, way, t, pl.ds(half_row, n)]
        else:
            dst = rel1.at[half, way, t, pl.ds(quarter_row, n)]
        return remote(
            part.at[zt, yt, pl.ds(hall_row, n)],
            dst,
            sends.at[2],
            (l1 if landing else r1).at[g, half, t],
            ring(half, 0)[1 + way],
        )

    def neighbour1(g, half, way, target, t):
        hall_row, half_row, _, n = rows_of(g, half, 0)
        skip = (1 - way) * n
        zt, yt = (t, target) if half == 0 else (target, t)
        peer = (aux, z * SIDE + target) if half == 0 else (aux, target * SIDE + y)
        return remote(
            part.at[zt, yt, pl.ds(pl.multiple_of(hall_row + skip, 32), n)],
            in1.at[half, way, t, pl.ds(pl.multiple_of(half_row + skip, 32), n)],
            sends.at[2],
            l1.at[g, half, t],
            peer,
        )

    def message2(g, half, j, target):
        which, way, landing = KINDS[j]
        _, half_row, quarter_row, n = rows_of(g, half, which)
        if landing:
            dst = in2.at[half, way, pl.ds(half_row, n)]
        else:
            dst = rel2.at[half, way, pl.ds(quarter_row, n)]
        return remote(
            tsum.at[half, target, pl.ds(half_row, n)],
            dst,
            sends.at[3],
            (l2 if landing else r2).at[g, half],
            ring(half, 1)[1 + way],
        )

    def wait1(g, half, t, landing):
        _, half_row, quarter_row, n = rows_of(g, half, 0)
        if landing:
            ref, sem = in1.at[half, :, t, pl.ds(half_row, 2 * n)], l1.at[g, half, t]
        else:
            ref, sem = rel1.at[half, :, t, pl.ds(quarter_row, n)], r1.at[g, half, t]
        remote(ref, ref, sends.at[2], sem, ring(half, 0)[1]).wait_recv()

    def wait2(g, half, landing):
        _, half_row, quarter_row, n = rows_of(g, half, 0)
        if landing:
            ref, sem = in2.at[half, :, pl.ds(half_row, 2 * n)], l2.at[g, half]
        else:
            ref, sem = rel2.at[half, :, pl.ds(quarter_row, n)], r2.at[g, half]
        remote(ref, ref, sends.at[3], sem, ring(half, 1)[1]).wait_recv()

    def at(here, delta):
        return (here + delta) % SIDE

    def blocks(n, body):
        def step(i, _):
            body(i * 32)
            return 0

        lax.fori_loop(0, n // 32, step, 0)

    def rows32(start, i):
        return pl.ds(pl.multiple_of(start + i, 32), 32)

    def relay1(g, half, delta):
        here = ring(half, 0)[0]
        t = at(z if half == 0 else y, delta)
        wait1(g, half, t, False)
        for way, onward, step in ((0, 3, 1), (1, 5, 3)):
            target = at(here, step)
            zt, yt = (t, target) if half == 0 else (target, t)
            hall_row, _, quarter_row, n = rows_of(g, half, way)

            def body(i):
                total = part[zt, yt, rows32(hall_row, i), :].astype(F32) + rel1[
                    half, way, t, rows32(quarter_row, i), :
                ].astype(F32)
                part[zt, yt, rows32(hall_row, i), :] = total.astype(BF16)

            blocks(n, body)
            message1(g, half, onward, target, t).start()

    def middle(g, half, delta):
        t = at(z if half == 0 else y, delta)
        wait1(g, half, t, True)
        zt, yt = (t, y) if half == 0 else (z, t)
        hall_row, half_row, _, n = rows_of(g, half, 0, 2)

        def body(i):
            total = (
                part[zt, yt, rows32(hall_row, i), :].astype(F32)
                + in1[half, 0, t, rows32(half_row, i), :].astype(F32)
                + in1[half, 1, t, rows32(half_row, i), :].astype(F32)
            )
            if delta:
                tsum[half, t, rows32(half_row, i), :] = total.astype(BF16)
            else:
                own[half, rows32(half_row, i), :] = total

        blocks(n, body)
        for j in {0: (), 1: (2,), 2: (0, 1), 3: (4,)}[delta]:
            message2(g, half, j, t).start()

    def relay2(g, half):
        here = ring(half, 1)[0]
        wait2(g, half, False)
        for way, onward, step in ((0, 3, 1), (1, 5, 3)):
            target = at(here, step)
            _, half_row, quarter_row, n = rows_of(g, half, way)

            def body(i):
                total = tsum[half, target, rows32(half_row, i), :].astype(F32) + rel2[
                    half, way, rows32(quarter_row, i), :
                ].astype(F32)
                tsum[half, target, rows32(half_row, i), :] = total.astype(BF16)

            blocks(n, body)
            message2(g, half, onward, target).start()

    def finish(g, half):
        wait2(g, half, True)
        hall_row, half_row, _, n = rows_of(g, half, 0, 2)

        def body(i):
            rows = rows32(half_row, i)
            total = (
                own[half, rows, :]
                + in2[half, 0, rows, :].astype(F32)
                + in2[half, 1, rows, :].astype(F32)
            )
            row = hall_row + i
            position = row // 128
            chip = (x + position + position // 2 - 2 * (position // 3)) % SIDE
            out_ref[rows32(chip * 128, row % 128), :] = total.astype(BF16)

        blocks(n, body)

    def compute(g, services):
        r0, rows = GROUPS[g]

        def body(i, carry):
            deltas_y, deltas_z = carry
            dy, dz = deltas_y % SIDE, deltas_z % SIDE
            yt, zt = at(y, dy), at(z, dz)
            column = pl.multiple_of((zt * SIDE + yt) * TILE, TILE)
            acc = jnp.dot(
                hall[pl.ds(r0, rows), :], virt[:, pl.ds(column, TILE)], preferred_element_type=F32
            )
            part[zt, yt, pl.ds(r0, rows), :] = acc.astype(BF16)
            for half, d, target, t in ((0, dy, yt, zt), (1, dz, zt, yt)):

                @pl.when(d == 2)
                def _():
                    message1(g, half, 0, target, t).start()
                    message1(g, half, 1, target, t).start()

                @pl.when(d % 2 == 1)
                def _():
                    neighbour1(g, half, d // 2, target, t).start()

            @pl.when(i % 2 == 1)
            def _():
                services(i)

            return deltas_y // SIDE, deltas_z // SIDE

        lax.fori_loop(
            0,
            SIDE * SIDE,
            body,
            (
                jnp.int32(sum(d << (2 * i) for i, (d, _) in enumerate(ORDER))),
                jnp.int32(sum(d << (2 * i) for i, (_, d) in enumerate(ORDER))),
            ),
        )

    def both(function, g, *rest):
        for half in range(2):
            function(g, half, *rest)

    def loop(n, function):
        lax.fori_loop(0, n, function, 0)

    def scoped(name, function):
        def run():
            with jax.named_scope(name):
                function()

        return run

    def when(condition, name, function):
        pl.when(condition)(scoped(name, function))

    with jax.named_scope("t_part0"):
        all_arrived(0, 0)
    with jax.named_scope("t_virt"):
        for copy in virt_copies:
            copy.wait()

    def services0(i):
        when(i < 8, "t_near", lambda: forward_near(i // 2, 0))
        when(i == 13, "t_far", lambda: loop(PIECES, forward_far))

    with jax.named_scope("t_C0"):
        compute(0, services0)
    with jax.named_scope("t_relay0"):
        for delta in range(SIDE):
            both(relay1, 0, delta)
    with jax.named_scope("t_part1"):
        all_arrived(3, 2)
        all_arrived(4, 1)
        all_arrived(6, 3)

    def middle0():
        for delta in (2, 1, 3, 0):
            both(middle, 0, delta)

    def relays():
        for delta in (1, 3):
            both(relay1, 1, delta)

    def services1(i):
        when(i == 5, "t_mid0", middle0)
        when(i == 9, "t_rel2", lambda: both(relay1, 1, 2))
        when(i == 11, "t_relay20", lambda: both(relay2, 0))
        when(i == 13, "t_rel13", relays)
        when(i == 15, "t_mid2", lambda: both(middle, 1, 2))

    with jax.named_scope("t_C1"):
        compute(1, services1)
    with jax.named_scope("t_rel0"):
        both(relay1, 1, 0)
    with jax.named_scope("t_mid1"):
        both(middle, 1, 1)
    with jax.named_scope("t_mid3"):
        both(middle, 1, 3)
    with jax.named_scope("t_relay21"):
        both(relay2, 1)
    with jax.named_scope("t_fin0"):
        both(finish, 0)
    with jax.named_scope("t_midown"):
        both(middle, 1, 0)
    with jax.named_scope("t_fin1"):
        both(finish, 1)

    with jax.named_scope("t_sends"):
        for j, ref in enumerate(
            (halo, hall.at[pl.ds(0, 448)], part.at[pl.ds(0, 3)], part.at[0, pl.ds(0, 3)])
        ):
            remote(ref, ref, sends.at[j], hr.at[0], partner).wait_send()


def local(v_blocks, pair_map, pair_count, occ_coef, virt_coef):
    anywhere = pl.BlockSpec(memory_space=pl.ANY)
    groups = len(GROUPS)
    rows_first = pl.pallas_call(
        kernel,
        out_shape=jax.ShapeDtypeStruct((512, TILE), BF16),
        in_specs=[anywhere] * 5,
        out_specs=pl.BlockSpec(memory_space=pltpu.VMEM),
        scratch_shapes=[
            pltpu.SMEM((1, 2, PAIR_CAP), jnp.int32),
            pltpu.SMEM((1, 1), jnp.int32),
            pltpu.VMEM((Q, PAIR_CAP, BB, BB), BF16),
            pltpu.VMEM((ROWS, COLS), BF16),
            pltpu.VMEM((NOCC, ROWS), BF16),
            pltpu.VMEM((2, NOCC, NEAR * BB), BF16),
            pltpu.VMEM((HERE + 2 * NEAR, NOCC, BB), F32),
            pltpu.VMEM((BB, PAIR_CAP * BB), BF16),
            pltpu.VMEM((512, ROWS), BF16),
            pltpu.VMEM((SIDE, SIDE, 512, TILE), BF16),
            pltpu.VMEM((2, 2, SIDE, 128, TILE), BF16),
            pltpu.VMEM((2, 2, SIDE, 256, TILE), BF16),
            pltpu.VMEM((2, SIDE, 256, TILE), BF16),
            pltpu.VMEM((2, 256, TILE), F32),
            pltpu.VMEM((2, 2, 128, TILE), BF16),
            pltpu.VMEM((2, 2, 256, TILE), BF16),
            pltpu.SemaphoreType.DMA((3,)),
            pltpu.SemaphoreType.DMA((PIECES,)),
            pltpu.SemaphoreType.DMA((SIDE,)),
            pltpu.SemaphoreType.DMA((4,)),
            pltpu.SemaphoreType.DMA((2,)),
            pltpu.SemaphoreType.DMA((3, PIECES)),
            pltpu.SemaphoreType.DMA((4,)),
            pltpu.SemaphoreType.DMA((groups, 2, SIDE)),
            pltpu.SemaphoreType.DMA((groups, 2, SIDE)),
            pltpu.SemaphoreType.DMA((groups, 2)),
            pltpu.SemaphoreType.DMA((groups, 2)),
        ],
        compiler_params=pltpu.CompilerParams(
            collective_id=0, has_side_effects=True, vmem_limit_bytes=60 << 20
        ),
        name="occupied_batch",
    )(jnp.swapaxes(pair_map, 1, 2), pair_count, v_blocks, occ_coef, virt_coef)
    return rows_first.T


def solution(mesh):
    in_specs = (
        P("aux", "basis", None, None),
        P("aux", "basis", None),
        P("aux", "basis"),
        P(None, "basis"),
        P("basis", "aux"),
    )
    out_specs = P(("aux", "basis"), None)
    return jax.shard_map(local, mesh=mesh, in_specs=in_specs, out_specs=out_specs, check_vma=False)
```

```python
import functools

import jax
import jax.numpy as jnp
from jax import lax
from jax.experimental import pallas as pl
from jax.experimental.pallas import tpu as pltpu
from jax.sharding import PartitionSpec as P

BB = 128
NOCC = 8
NEAR = 8
PAIR_CAP = 48
NB = 240
Q = 8
HERE = 15
ROWS = HERE * BB
COLS = 4096
TILE = 256
SIDE = 4
PIECES = 4
GROUPS = ((0, 128), (128, 384))
ORDER0 = (
    (2, 2), (1, 2), (3, 2), (0, 2), (2, 1), (2, 3), (2, 0), (1, 1),
    (3, 1), (0, 1), (1, 3), (3, 3), (0, 3), (1, 0), (3, 0), (0, 0),
)
ORDER1 = (
    (2, 2), (1, 2), (2, 1), (3, 2), (2, 3), (1, 1), (3, 3), (1, 3),
    (3, 1), (0, 2), (2, 0), (0, 1), (1, 0), (0, 3), (3, 0), (0, 0),
)
MESH = pl.DeviceIdType.MESH
F32 = jnp.float32
BF16 = jnp.bfloat16


def kernel(
    pm_hbm,
    pc_hbm,
    v_hbm,
    occ_hbm,
    virt_hbm,
    out_hbm,
    out_ref,
    pm,
    pc,
    v,
    virt,
    occ,
    halo,
    tab,
    lhs,
    hall,
    part,
    rel0,
    in0,
    in1,
    tsum,
    own,
    rel2,
    in2,
    isem,
    vsem,
    wsem,
    sends,
    hr,
    gr,
    gr_all,
    m0,
    m1,
    m2,
):
    aux = lax.axis_index("aux")
    basis = lax.axis_index("basis")
    x, c = aux // 2, aux % 2
    z, y = basis // SIDE, basis % SIDE

    partner = (2 * x + 1 - c, basis)
    x_up = (2 * ((x + 1) % SIDE) + c, basis)
    x_down = (2 * ((x + 3) % SIDE) + c, basis)
    y_up = (aux, z * SIDE + (y + 1) % SIDE)
    y_down = (aux, z * SIDE + (y + 3) % SIDE)
    z_up = (aux, ((z + 1) % SIDE) * SIDE + y)
    z_down = (aux, ((z + 3) % SIDE) * SIDE + y)
    b_up = (aux, (basis + 1) % (SIDE * SIDE))
    b_down = (aux, (basis + SIDE * SIDE - 1) % (SIDE * SIDE))
    x_relay = (2 * ((x + 1 + 2 * c) % SIDE) + c, basis)

    barrier = pltpu.get_barrier_semaphore()
    peers = (b_up, b_down, z_up, z_down, y_up, y_down, x_up, x_down, partner)
    for peer in peers:
        pl.semaphore_signal(
            barrier, inc=1, device_id={"aux": peer[0], "basis": peer[1]}, device_id_type=MESH
        )

    def remote(src, dst, send, recv, peer):
        return pltpu.make_async_remote_copy(
            src_ref=src,
            dst_ref=dst,
            send_sem=send,
            recv_sem=recv,
            device_id={"aux": peer[0], "basis": peer[1]},
            device_id_type=MESH,
        )

    small = (
        pltpu.make_async_copy(occ_hbm, occ, isem.at[0]),
        pltpu.make_async_copy(pm_hbm, pm, isem.at[1]),
        pltpu.make_async_copy(pc_hbm, pc, isem.at[2]),
    )
    for copy in small:
        copy.start()

    def v_copy(p):
        return pltpu.make_async_copy(v_hbm.at[pl.ds(2 * p, 2)], v.at[pl.ds(2 * p, 2)], vsem.at[p])

    def virt_copy(delta):
        columns = pl.ds(pl.multiple_of((z + delta) % SIDE * 1024, 1024), 1024)
        return pltpu.make_async_copy(
            virt_hbm.at[:, columns], virt.at[:, columns], wsem.at[delta]
        )

    for p in range(PIECES):
        v_copy(p).start()
    for delta in (2, 1, 3, 0):
        virt_copy(delta).start()
    with jax.named_scope("t_barrier"):
        pl.semaphore_wait(barrier, len(peers))

    width = NEAR * BB
    with jax.named_scope("t_occ"):
        small[0].wait()
    to_up = remote(occ.at[:, pl.ds(ROWS - width, width)], halo.at[0], sends.at[0], hr.at[0], b_up)
    to_down = remote(occ.at[:, pl.ds(0, width)], halo.at[1], sends.at[0], hr.at[1], b_down)
    to_up.start()
    to_down.start()
    for j in range(HERE):
        tab[NEAR + j] = occ[:, j * BB : (j + 1) * BB].astype(F32)
    with jax.named_scope("t_halo"):
        to_up.wait_recv()
        to_down.wait_recv()
    with jax.named_scope("t_small"):
        small[1].wait()
        small[2].wait()
    for j in range(NEAR):
        tab[j] = halo[0, :, j * BB : (j + 1) * BB].astype(F32)
        tab[NEAR + HERE + j] = halo[1, :, j * BB : (j + 1) * BB].astype(F32)

    first = basis * HERE
    row_block = lax.broadcasted_iota(jnp.int32, (BB, BB), 0) // NOCC

    def build(k, _):
        mu = pm[0, 0, k]
        nu = pm[0, 1, k]
        place = jnp.where(k < pc[0, 0], mu - first, -1)
        pos = jnp.clip(lax.rem(nu - first + NEAR + NB, NB), 0, HERE + 2 * NEAR - 1)
        stack = jnp.concatenate([tab[pos]] * (BB // NOCC), axis=0)
        lhs[:, pl.ds(pl.multiple_of(k * BB, BB), BB)] = jnp.where(
            row_block == place, stack, 0.0
        ).astype(BF16)
        return 0

    with jax.named_scope("t_build"):
        lax.fori_loop(0, PAIR_CAP, build, 0, unroll=4)

    def piece_ref(position, core, p):
        return hall.at[pl.ds(pl.multiple_of(position * 128 + core * 64 + p * 16, 16), 16)]

    def gather_sem(message, p):
        if message in (1, 2, 5):
            return gr.at[(1, 2, 5).index(message), p]
        return gr_all.at[(0, 3, 4, 6).index(message)]

    def gather(message, p, position_src, position_dst, core, peer):
        return remote(
            piece_ref(position_src, core, p),
            piece_ref(position_dst, core, p),
            sends.at[1],
            gather_sem(message, p),
            peer,
        )

    def arrived(message, p, position, core, peer):
        ref = piece_ref(position, core, p)
        remote(ref, ref, sends.at[1], gather_sem(message, p), peer).wait_recv()

    def all_arrived(message, position):
        ref = hall.at[pl.ds(pl.multiple_of(position * 128 + (1 - c) * 64, 64), 64)]
        remote(ref, ref, sends.at[1], gather_sem(message, 0), partner).wait_recv()

    def first_half(p, _):
        v_copy(p).wait()
        acc = jnp.zeros((BB, 2 * BB), F32)
        for k in range(0, PAIR_CAP, 2):
            w = jnp.concatenate(
                [
                    jnp.concatenate([v[2 * p + e, k], v[2 * p + e, k + 1]], axis=1)
                    for e in range(2)
                ],
                axis=0,
            )
            acc += lax.dot_general(
                lhs[:, k * BB : (k + 2) * BB],
                w,
                (((1,), (1,)), ((), ())),
                preferred_element_type=F32,
            )
        row = pl.multiple_of(c * 64 + p * 16, 16)
        for j in range(HERE):
            lines = acc[j * NOCC : (j + 1) * NOCC]
            both = jnp.concatenate([lines[:, :BB], lines[:, BB:]], axis=0)
            hall[pl.ds(row, 16), j * BB : (j + 1) * BB] = both.astype(BF16)
        gather(0, p, 0, 0, c, partner).start()
        gather(1, p, 0, 2, c, x_up).start()
        gather(2, p, 0, 1, c, x_down).start()
        return 0

    with jax.named_scope("t_first"):
        lax.fori_loop(0, PIECES, first_half, 0)

    def forward_near(p, _):
        arrived(1, p, 2, c, x_down)
        gather(3, p, 2, 2, c, partner).start()
        arrived(2, p, 1, c, x_up)
        gather(4, p, 1, 1, c, partner).start()
        gather(5, p, 2 - c, 3, c, x_relay).start()
        return 0

    def forward_far(p, _):
        arrived(5, p, 3, c, x_relay)
        gather(6, p, 3, 3, c, partner).start()
        return 0

    def rows_of(g, half, which, count=1):
        r0, rows = GROUPS[g]
        quarter = rows // 4
        return (
            r0 + half * 2 * quarter + which * quarter,
            r0 // 2 + which * quarter,
            r0 // 4,
            quarter * count,
        )

    def ring(half, phase):
        return (y, y_up, y_down) if half == phase else (z, z_up, z_down)

    def at(here, delta):
        return (here + delta) % SIDE

    KINDS = ((0, 0, 0), (1, 1, 0), (1, 0, 1), (0, 0, 1), (0, 1, 1), (1, 1, 1))

    def bulk(half, j, target):
        which, way, landing = KINDS[j]
        hall_row, half_row, quarter_row, n = rows_of(0, half, which)
        rows = pl.ds(hall_row, n)
        return remote(
            part.at[:, target, rows] if half == 0 else part.at[target, :, rows],
            in0.at[half, way, :, pl.ds(half_row, n)] if landing else rel0.at[half, way],
            sends.at[2],
            m0.at[landing, half],
            ring(half, 0)[1 + way],
        )

    R0, RN = GROUPS[1]
    QUARTER = RN // 4

    def single(half, which, way, landing, target, t):
        put = which * QUARTER if landing else 2 * QUARTER
        zt, yt = (t, target) if half == 0 else (target, t)
        return remote(
            part.at[zt, yt, pl.ds(R0 + (2 * half + which) * QUARTER, QUARTER)],
            in1.at[half, way, t, pl.ds(put, QUARTER)],
            sends.at[2],
            m1.at[landing, half, t],
            ring(half, 0)[1 + way],
        )

    def send_chunk(dy, dz):
        yt, zt = at(y, dy), at(z, dz)
        for half, d, target, t in ((0, dy, yt, zt), (1, dz, zt, yt)):
            if d == 2:
                single(half, 0, 0, 0, target, t).start()
                single(half, 1, 1, 0, target, t).start()
            elif d:
                single(half, 1 - d // 2, d // 2, 1, target, t).start()

    def message2(g, half, j, target):
        which, way, landing = KINDS[j]
        _, half_row, quarter_row, n = rows_of(g, half, which)
        if landing:
            dst = in2.at[half, way, pl.ds(half_row, n)]
        else:
            dst = rel2.at[half, way, pl.ds(quarter_row, n)]
        return remote(
            tsum.at[half, target, pl.ds(half_row, n)],
            dst,
            sends.at[3],
            m2.at[landing, g, half],
            ring(half, 1)[1 + way],
        )

    def wait1(half, t, landing):
        rows = pl.ds(0, 2 * QUARTER) if landing else pl.ds(2 * QUARTER, QUARTER)
        ref = in1.at[half, :, t, rows]
        remote(ref, ref, sends.at[2], m1.at[landing, half, t], ring(half, 0)[1]).wait_recv()

    def wait0(half, landing):
        ref = in0.at[half] if landing else rel0.at[half]
        remote(ref, ref, sends.at[2], m0.at[landing, half], ring(half, 0)[1]).wait_recv()

    def wait2(g, half, landing):
        _, half_row, quarter_row, n = rows_of(g, half, 0)
        if landing:
            ref = in2.at[half, :, pl.ds(half_row, 2 * n)]
        else:
            ref = rel2.at[half, :, pl.ds(quarter_row, n)]
        remote(ref, ref, sends.at[3], m2.at[landing, g, half], ring(half, 1)[1]).wait_recv()

    def blocks(n, body):
        def step(i, _):
            body(i * 32)
            return 0

        lax.fori_loop(0, n // 32, step, 0)

    def rows32(start, i):
        return pl.ds(pl.multiple_of(start + i, 32), 32)

    def relay1(half, delta):
        here = ring(half, 0)[0]
        t = at(z if half == 0 else y, delta)
        wait1(half, t, 0)
        for way, step in ((0, 1), (1, 3)):
            target = at(here, step)
            zt, yt = (t, target) if half == 0 else (target, t)
            row = R0 + (2 * half + way) * QUARTER

            def body(i):
                total = part[zt, yt, rows32(row, i), :].astype(F32) + in1[
                    half, way, t, rows32(2 * QUARTER, i), :
                ].astype(F32)
                part[zt, yt, rows32(row, i), :] = total.astype(BF16)

            blocks(QUARTER, body)
            single(half, way, way, 1, target, t).start()

    def relay0(half):
        here = ring(half, 0)[0]
        wait0(half, 0)
        for way, onward, step in ((0, 3, 1), (1, 5, 3)):
            target = at(here, step)
            row, _, _, n = rows_of(0, half, way)

            def body(t, _):
                zt, yt = (t, target) if half == 0 else (target, t)
                total = part[zt, yt, pl.ds(row, n), :].astype(F32) + rel0[half, way, t].astype(F32)
                part[zt, yt, pl.ds(row, n), :] = total.astype(BF16)
                return 0

            lax.fori_loop(0, SIDE, body, 0)
            bulk(half, onward, target).start()

    def middle(g, half, delta):
        t = at(z if half == 0 else y, delta)
        if g:
            wait1(half, t, 1)
        zt, yt = (t, y) if half == 0 else (z, t)
        hall_row, half_row, _, n = rows_of(g, half, 0, 2)
        landed = in1 if g else in0

        def body(i):
            total = (
                part[zt, yt, rows32(hall_row, i), :].astype(F32)
                + landed[half, 0, t, rows32(0, i), :].astype(F32)
                + landed[half, 1, t, rows32(0, i), :].astype(F32)
            )
            if delta:
                tsum[half, t, rows32(half_row, i), :] = total.astype(BF16)
            else:
                own[half, rows32(half_row, i), :] = total

        blocks(n, body)
        for j in {0: (), 1: (2,), 2: (0, 1), 3: (4,)}[delta]:
            message2(g, half, j, t).start()

    def relay2(g, half):
        here = ring(half, 1)[0]
        wait2(g, half, 0)
        for way, onward, step in ((0, 3, 1), (1, 5, 3)):
            target = at(here, step)
            _, half_row, quarter_row, n = rows_of(g, half, way)

            def body(i):
                total = tsum[half, target, rows32(half_row, i), :].astype(F32) + rel2[
                    half, way, rows32(quarter_row, i), :
                ].astype(F32)
                tsum[half, target, rows32(half_row, i), :] = total.astype(BF16)

            blocks(n, body)
            message2(g, half, onward, target).start()

    def finish(g, half):
        wait2(g, half, 1)
        hall_row, half_row, _, n = rows_of(g, half, 0, 2)

        def body(i):
            rows = rows32(half_row, i)
            total = (
                own[half, rows, :]
                + in2[half, 0, rows, :].astype(F32)
                + in2[half, 1, rows, :].astype(F32)
            )
            row = hall_row + i
            position = row // 128
            chip = (x + position + position // 2 - 2 * (position // 3)) % SIDE
            out_ref[rows32(chip * 128, row % 128), :] = total.astype(BF16)

        blocks(n, body)

    def compute(g, order, segments, bounds, services):
        r0, rows = GROUPS[g]

        def product(_, carry):
            deltas_y, deltas_z = carry
            yt, zt = at(y, deltas_y % SIDE), at(z, deltas_z % SIDE)
            column = pl.multiple_of((zt * SIDE + yt) * TILE, TILE)
            acc = jnp.dot(
                hall[pl.ds(r0, rows), :], virt[:, pl.ds(column, TILE)], preferred_element_type=F32
            )
            part[zt, yt, pl.ds(r0, rows), :] = acc.astype(BF16)
            return deltas_y // SIDE, deltas_z // SIDE

        def segment(s, carry):
            low, high = bounds(s)
            after = lax.fori_loop(low, high, product, carry)
            services(s)
            return after

        packed = [
            jnp.int32(sum(pair[k] << (2 * i) for i, pair in enumerate(order))) for k in range(2)
        ]
        lax.fori_loop(0, segments, segment, tuple(packed))

    def both(function, *rest):
        for half in range(2):
            function(*rest[:1], half, *rest[1:])

    def loop(n, function):
        lax.fori_loop(0, n, function, 0)

    def scoped(name, function):
        def run():
            with jax.named_scope(name):
                function()

        return run

    def when(condition, name, function):
        pl.when(condition)(scoped(name, function))

    with jax.named_scope("t_near0"):
        forward_near(0, 0)
    with jax.named_scope("t_part0"):
        all_arrived(0, 0)
    with jax.named_scope("t_virt"):
        virt_copy(2).wait()

    def starts(half, *messages):
        here = ring(half, 0)[0]

        def run():
            for j in messages:
                bulk(half, j, at(here, (2, 2, 1, 1, 3, 3)[j])).start()

        return run

    def services0(s):
        when(
            s == 0,
            "t_s0",
            lambda: (
                starts(1, 0, 1)(),
                [virt_copy(delta).wait() for delta in (1, 3, 0)],
                forward_near(1, 0),
                forward_near(2, 0),
            ),
        )
        when(s == 1, "t_s1", lambda: (starts(0, 0, 1)(), forward_near(3, 0)))
        when(s == 2, "t_s2", lambda: (starts(1, 2)(), loop(1, forward_far)))
        when(s == 3, "t_s3", lambda: (starts(1, 4)(), forward_far(1, 0), forward_far(2, 0)))
        when(s == 4, "t_s4", starts(0, 2, 4))

    with jax.named_scope("t_C0"):
        compute(0, ORDER0, 5, lambda s: (jnp.where(s == 0, 0, 1 + 3 * s), 4 + 3 * s), services0)
    with jax.named_scope("t_far23"):
        forward_far(3, 0)
    with jax.named_scope("t_relay0"):
        relay0(0)
        relay0(1)
    with jax.named_scope("t_part1"):
        all_arrived(3, 2)
        all_arrived(4, 1)
        all_arrived(6, 3)

    def middle0():
        for half in range(2):
            wait0(half, 1)
            for delta in (2, 1, 3, 0):
                middle(0, half, delta)

    def relays(*deltas):
        for delta in deltas:
            for half in range(2):
                relay1(half, delta)

    def bounds1(s):
        return jnp.where(s < 2, s, 2 * s - 2), jnp.where(s < 2, s + 1, 2 * s)

    then1 = {
        3: lambda: relays(2),
        5: lambda: relays(1, 3),
        6: lambda: both(middle, 1, 2),
        8: middle0,
    }

    def services1(s):
        def run(k):
            def go():
                for i in (k,) if k < 2 else (2 * k - 2, 2 * k - 1):
                    send_chunk(*ORDER1[i])
                if k in then1:
                    with jax.named_scope(f"t_then{k}"):
                        then1[k]()

            return go

        @pl.when(s < 4)
        def _():
            for k in range(4):
                when(s == k, f"t_s1{k}", run(k))

        @pl.when(s >= 4)
        def _():
            for k in range(4, 9):
                when(s == k, f"t_s1{k}", run(k))

    with jax.named_scope("t_C1"):
        compute(1, ORDER1, 9, bounds1, services1)
    with jax.named_scope("t_rel0"):
        relays(0)
    with jax.named_scope("t_mid13"):
        both(middle, 1, 1)
        both(middle, 1, 3)
    with jax.named_scope("t_relay21"):
        both(relay2, 1)
    with jax.named_scope("t_relay20"):
        both(relay2, 0)
    with jax.named_scope("t_midown"):
        both(middle, 1, 0)
    with jax.named_scope("t_fin1"):
        both(finish, 1)
    with jax.named_scope("t_fin0"):
        both(finish, 0)
    with jax.named_scope("t_out"):
        out_copy = pltpu.make_async_copy(out_ref, out_hbm, isem.at[0])
        out_copy.start()
        out_copy.wait()

    with jax.named_scope("t_sends"):
        for j, ref in enumerate(
            (halo, hall.at[pl.ds(0, 448)], part.at[pl.ds(0, 3)], part.at[0, pl.ds(0, 3)])
        ):
            remote(ref, ref, sends.at[j], hr.at[0], partner).wait_send()


def local(v_blocks, pair_map, pair_count, occ_coef, virt_coef):
    anywhere = pl.BlockSpec(memory_space=pl.ANY)
    groups = len(GROUPS)
    rows_first = pl.pallas_call(
        kernel,
        out_shape=jax.ShapeDtypeStruct((512, TILE), BF16),
        in_specs=[pl.BlockSpec(memory_space=pltpu.HBM)] * 5,
        out_specs=anywhere,
        scratch_shapes=[
            pltpu.VMEM((512, TILE), BF16),
            pltpu.SMEM((1, 2, PAIR_CAP), jnp.int32),
            pltpu.SMEM((1, 1), jnp.int32),
            pltpu.VMEM((Q, PAIR_CAP, BB, BB), BF16),
            pltpu.VMEM((ROWS, COLS), BF16),
            pltpu.VMEM((NOCC, ROWS), BF16),
            pltpu.VMEM((2, NOCC, NEAR * BB), BF16),
            pltpu.VMEM((HERE + 2 * NEAR, NOCC, BB), F32),
            pltpu.VMEM((BB, PAIR_CAP * BB), BF16),
            pltpu.VMEM((512, ROWS), BF16),
            pltpu.VMEM((SIDE, SIDE, 512, TILE), BF16),
            pltpu.VMEM((2, 2, SIDE, 32, TILE), BF16),
            pltpu.VMEM((2, 2, SIDE, 64, TILE), BF16),
            pltpu.VMEM((2, 2, SIDE, 288, TILE), BF16),
            pltpu.VMEM((2, SIDE, 256, TILE), BF16),
            pltpu.VMEM((2, 256, TILE), F32),
            pltpu.VMEM((2, 2, 128, TILE), BF16),
            pltpu.VMEM((2, 2, 256, TILE), BF16),
            pltpu.SemaphoreType.DMA((3,)),
            pltpu.SemaphoreType.DMA((PIECES,)),
            pltpu.SemaphoreType.DMA((SIDE,)),
            pltpu.SemaphoreType.DMA((4,)),
            pltpu.SemaphoreType.DMA((2,)),
            pltpu.SemaphoreType.DMA((3, PIECES)),
            pltpu.SemaphoreType.DMA((4,)),
            pltpu.SemaphoreType.DMA((2, 2)),
            pltpu.SemaphoreType.DMA((2, 2, SIDE)),
            pltpu.SemaphoreType.DMA((2, groups, 2)),
        ],
        compiler_params=pltpu.CompilerParams(
            collective_id=0, has_side_effects=True, vmem_limit_bytes=44 << 20
        ),
        name="occupied_batch",
    )(jnp.swapaxes(pair_map, 1, 2), pair_count, v_blocks, occ_coef, virt_coef)
    return rows_first.T


def solution(mesh):
    in_specs = (
        P("aux", "basis", None, None),
        P("aux", "basis", None),
        P("aux", "basis"),
        P(None, "basis"),
        P("basis", "aux"),
    )
    out_specs = P(("aux", "basis"), None)
    return jax.shard_map(local, mesh=mesh, in_specs=in_specs, out_specs=out_specs, check_vma=False)
```

```python
import functools

import jax
import jax.numpy as jnp
from jax import lax
from jax.experimental import pallas as pl
from jax.experimental.pallas import tpu as pltpu
from jax.sharding import PartitionSpec as P

BB = 128
NOCC = 8
NEAR = 8
PAIR_CAP = 48
NB = 240
Q = 8
HERE = 15
ROWS = HERE * BB
COLS = 4096
TILE = 256
SIDE = 4
PIECES = 4
GROUPS = ((0, 128), (128, 384))
ORDER0 = (
    (2, 2), (1, 2), (3, 2), (0, 2), (2, 1), (2, 3), (2, 0), (1, 1),
    (3, 1), (0, 1), (1, 3), (3, 3), (0, 3), (1, 0), (3, 0), (0, 0),
)
ORDER1 = (
    (2, 2), (1, 2), (2, 1), (3, 2), (2, 3), (1, 1), (3, 3), (1, 3),
    (3, 1), (0, 2), (2, 0), (0, 1), (1, 0), (0, 3), (3, 0), (0, 0),
)
MESH = pl.DeviceIdType.MESH
F32 = jnp.float32
BF16 = jnp.bfloat16


def kernel(
    pm_hbm,
    pc_hbm,
    v_hbm,
    occ_hbm,
    virt_hbm,
    out_hbm,
    out_ref,
    pm,
    pc,
    v,
    virt,
    occ,
    halo,
    tab,
    lhs,
    hall,
    part,
    rel0,
    in0,
    in1,
    tsum,
    own,
    rel2,
    in2,
    isem,
    vsem,
    wsem,
    sends,
    hr,
    gr,
    gr_all,
    m0,
    m1,
    m2,
):
    aux = lax.axis_index("aux")
    basis = lax.axis_index("basis")
    x, c = aux // 2, aux % 2
    z, y = basis // SIDE, basis % SIDE

    partner = (2 * x + 1 - c, basis)
    x_up = (2 * ((x + 1) % SIDE) + c, basis)
    x_down = (2 * ((x + 3) % SIDE) + c, basis)
    y_up = (aux, z * SIDE + (y + 1) % SIDE)
    y_down = (aux, z * SIDE + (y + 3) % SIDE)
    z_up = (aux, ((z + 1) % SIDE) * SIDE + y)
    z_down = (aux, ((z + 3) % SIDE) * SIDE + y)
    b_up = (aux, (basis + 1) % (SIDE * SIDE))
    b_down = (aux, (basis + SIDE * SIDE - 1) % (SIDE * SIDE))
    x_relay = (2 * ((x + 1 + 2 * c) % SIDE) + c, basis)

    barrier = pltpu.get_barrier_semaphore()
    peers = (b_up, b_down, z_up, z_down, y_up, y_down, x_up, x_down, partner)
    for peer in peers:
        pl.semaphore_signal(
            barrier, inc=1, device_id={"aux": peer[0], "basis": peer[1]}, device_id_type=MESH
        )

    def remote(src, dst, send, recv, peer):
        return pltpu.make_async_remote_copy(
            src_ref=src,
            dst_ref=dst,
            send_sem=send,
            recv_sem=recv,
            device_id={"aux": peer[0], "basis": peer[1]},
            device_id_type=MESH,
        )

    small = (
        pltpu.make_async_copy(occ_hbm, occ, isem.at[0]),
        pltpu.make_async_copy(pm_hbm, pm, isem.at[1]),
        pltpu.make_async_copy(pc_hbm, pc, isem.at[2]),
    )
    for copy in small:
        copy.start()

    def v_copy(p):
        return pltpu.make_async_copy(v_hbm.at[pl.ds(2 * p, 2)], v.at[pl.ds(2 * p, 2)], vsem.at[p])

    def virt_copy(delta):
        columns = pl.ds(pl.multiple_of((z + delta) % SIDE * 1024, 1024), 1024)
        return pltpu.make_async_copy(
            virt_hbm.at[:, columns], virt.at[:, columns], wsem.at[delta]
        )

    for p in range(PIECES):
        v_copy(p).start()
    with jax.named_scope("t_barrier"):
        pl.semaphore_wait(barrier, len(peers))

    width = NEAR * BB
    with jax.named_scope("t_occ"):
        small[0].wait()
    to_up = remote(occ.at[:, pl.ds(ROWS - width, width)], halo.at[0], sends.at[0], hr.at[0], b_up)
    to_down = remote(occ.at[:, pl.ds(0, width)], halo.at[1], sends.at[0], hr.at[1], b_down)
    to_up.start()
    to_down.start()
    for j in range(HERE):
        tab[NEAR + j] = occ[:, j * BB : (j + 1) * BB].astype(F32)
    with jax.named_scope("t_halo"):
        to_up.wait_recv()
        to_down.wait_recv()
    with jax.named_scope("t_small"):
        small[1].wait()
        small[2].wait()
    for delta in (2, 1, 3, 0):
        virt_copy(delta).start()
    for j in range(NEAR):
        tab[j] = halo[0, :, j * BB : (j + 1) * BB].astype(F32)
        tab[NEAR + HERE + j] = halo[1, :, j * BB : (j + 1) * BB].astype(F32)

    first = basis * HERE
    row_block = lax.broadcasted_iota(jnp.int32, (BB, BB), 0) // NOCC

    def build(k, _):
        mu = pm[0, 0, k]
        nu = pm[0, 1, k]
        place = jnp.where(k < pc[0, 0], mu - first, -1)
        pos = jnp.clip(lax.rem(nu - first + NEAR + NB, NB), 0, HERE + 2 * NEAR - 1)
        stack = jnp.concatenate([tab[pos]] * (BB // NOCC), axis=0)
        lhs[:, pl.ds(pl.multiple_of(k * BB, BB), BB)] = jnp.where(
            row_block == place, stack, 0.0
        ).astype(BF16)
        return 0

    with jax.named_scope("t_build"):
        lax.fori_loop(0, PAIR_CAP, build, 0, unroll=4)

    def piece_ref(position, core, p):
        return hall.at[pl.ds(pl.multiple_of(position * 128 + core * 64 + p * 16, 16), 16)]

    def gather_sem(message, p):
        if message in (1, 2, 5):
            return gr.at[(1, 2, 5).index(message), p]
        return gr_all.at[(0, 3, 4, 6).index(message)]

    def gather(message, p, position_src, position_dst, core, peer):
        return remote(
            piece_ref(position_src, core, p),
            piece_ref(position_dst, core, p),
            sends.at[1],
            gather_sem(message, p),
            peer,
        )

    def arrived(message, p, position, core, peer):
        ref = piece_ref(position, core, p)
        remote(ref, ref, sends.at[1], gather_sem(message, p), peer).wait_recv()

    def all_arrived(message, position):
        ref = hall.at[pl.ds(pl.multiple_of(position * 128 + (1 - c) * 64, 64), 64)]
        remote(ref, ref, sends.at[1], gather_sem(message, 0), partner).wait_recv()

    def first_half(p, _):
        v_copy(p).wait()
        acc = jnp.zeros((BB, 2 * BB), F32)
        for k in range(0, PAIR_CAP, 2):
            w = jnp.concatenate(
                [
                    jnp.concatenate([v[2 * p + e, k], v[2 * p + e, k + 1]], axis=1)
                    for e in range(2)
                ],
                axis=0,
            )
            acc += lax.dot_general(
                lhs[:, k * BB : (k + 2) * BB],
                w,
                (((1,), (1,)), ((), ())),
                preferred_element_type=F32,
            )
        row = pl.multiple_of(c * 64 + p * 16, 16)
        for j in range(HERE):
            lines = acc[j * NOCC : (j + 1) * NOCC]
            both = jnp.concatenate([lines[:, :BB], lines[:, BB:]], axis=0)
            hall[pl.ds(row, 16), j * BB : (j + 1) * BB] = both.astype(BF16)
        gather(0, p, 0, 0, c, partner).start()
        gather(1, p, 0, 2, c, x_up).start()
        gather(2, p, 0, 1, c, x_down).start()
        return 0

    with jax.named_scope("t_first"):
        lax.fori_loop(0, PIECES, first_half, 0)

    def forward_near(p, _):
        arrived(1, p, 2, c, x_down)
        gather(3, p, 2, 2, c, partner).start()
        arrived(2, p, 1, c, x_up)
        gather(4, p, 1, 1, c, partner).start()
        gather(5, p, 2 - c, 3, c, x_relay).start()
        return 0

    def forward_far(p, _):
        arrived(5, p, 3, c, x_relay)
        gather(6, p, 3, 3, c, partner).start()
        return 0

    def rows_of(g, half, which, count=1):
        r0, rows = GROUPS[g]
        quarter = rows // 4
        return (
            r0 + half * 2 * quarter + which * quarter,
            r0 // 2 + which * quarter,
            r0 // 4,
            quarter * count,
        )

    def ring(half, phase):
        return (y, y_up, y_down) if half == phase else (z, z_up, z_down)

    def at(here, delta):
        return (here + delta) % SIDE

    KINDS = ((0, 0, 0), (1, 1, 0), (1, 0, 1), (0, 0, 1), (0, 1, 1), (1, 1, 1))

    def bulk(half, j, target):
        which, way, landing = KINDS[j]
        hall_row, half_row, quarter_row, n = rows_of(0, half, which)
        rows = pl.ds(hall_row, n)
        return remote(
            part.at[:, target, rows] if half == 0 else part.at[target, :, rows],
            in0.at[half, way, :, pl.ds(half_row, n)] if landing else rel0.at[half, way],
            sends.at[2],
            m0.at[landing, half],
            ring(half, 0)[1 + way],
        )

    R0, RN = GROUPS[1]
    QUARTER = RN // 4

    def single(half, which, way, landing, target, t):
        put = which * QUARTER if landing else 2 * QUARTER
        zt, yt = (t, target) if half == 0 else (target, t)
        return remote(
            part.at[zt, yt, pl.ds(R0 + (2 * half + which) * QUARTER, QUARTER)],
            in1.at[half, way, t, pl.ds(put, QUARTER)],
            sends.at[2],
            m1.at[landing, half, t],
            ring(half, 0)[1 + way],
        )

    def send_chunk(dy, dz):
        yt, zt = at(y, dy), at(z, dz)
        for half, d, target, t in ((0, dy, yt, zt), (1, dz, zt, yt)):
            if d == 2:
                single(half, 0, 0, 0, target, t).start()
                single(half, 1, 1, 0, target, t).start()
            elif d:
                single(half, 1 - d // 2, d // 2, 1, target, t).start()

    def message2(g, half, j, target):
        which, way, landing = KINDS[j]
        _, half_row, quarter_row, n = rows_of(g, half, which)
        if landing:
            dst = in2.at[half, way, pl.ds(half_row, n)]
        else:
            dst = rel2.at[half, way, pl.ds(quarter_row, n)]
        return remote(
            tsum.at[half, target, pl.ds(half_row, n)],
            dst,
            sends.at[3],
            m2.at[landing, g, half],
            ring(half, 1)[1 + way],
        )

    def wait1(half, t, landing):
        rows = pl.ds(0, 2 * QUARTER) if landing else pl.ds(2 * QUARTER, QUARTER)
        ref = in1.at[half, :, t, rows]
        remote(ref, ref, sends.at[2], m1.at[landing, half, t], ring(half, 0)[1]).wait_recv()

    def wait0(half, landing):
        ref = in0.at[half] if landing else rel0.at[half]
        remote(ref, ref, sends.at[2], m0.at[landing, half], ring(half, 0)[1]).wait_recv()

    def wait2(g, half, landing):
        _, half_row, quarter_row, n = rows_of(g, half, 0)
        if landing:
            ref = in2.at[half, :, pl.ds(half_row, 2 * n)]
        else:
            ref = rel2.at[half, :, pl.ds(quarter_row, n)]
        remote(ref, ref, sends.at[3], m2.at[landing, g, half], ring(half, 1)[1]).wait_recv()

    def blocks(n, body):
        def step(i, _):
            body(i * 32)
            return 0

        lax.fori_loop(0, n // 32, step, 0)

    def rows32(start, i):
        return pl.ds(pl.multiple_of(start + i, 32), 32)

    def relay1(half, delta):
        here = ring(half, 0)[0]
        t = at(z if half == 0 else y, delta)
        wait1(half, t, 0)
        for way, step in ((0, 1), (1, 3)):
            target = at(here, step)
            zt, yt = (t, target) if half == 0 else (target, t)
            row = R0 + (2 * half + way) * QUARTER

            def body(i):
                total = part[zt, yt, rows32(row, i), :].astype(F32) + in1[
                    half, way, t, rows32(2 * QUARTER, i), :
                ].astype(F32)
                part[zt, yt, rows32(row, i), :] = total.astype(BF16)

            blocks(QUARTER, body)
            single(half, way, way, 1, target, t).start()

    def relay0(half):
        here = ring(half, 0)[0]
        wait0(half, 0)
        for way, onward, step in ((0, 3, 1), (1, 5, 3)):
            target = at(here, step)
            row, _, _, n = rows_of(0, half, way)

            def body(t, _):
                zt, yt = (t, target) if half == 0 else (target, t)
                total = part[zt, yt, pl.ds(row, n), :].astype(F32) + rel0[half, way, t].astype(F32)
                part[zt, yt, pl.ds(row, n), :] = total.astype(BF16)
                return 0

            lax.fori_loop(0, SIDE, body, 0)
            bulk(half, onward, target).start()

    def middle(g, half, delta):
        t = at(z if half == 0 else y, delta)
        if g:
            wait1(half, t, 1)
        zt, yt = (t, y) if half == 0 else (z, t)
        hall_row, half_row, _, n = rows_of(g, half, 0, 2)
        landed = in1 if g else in0

        def body(i):
            total = (
                part[zt, yt, rows32(hall_row, i), :].astype(F32)
                + landed[half, 0, t, rows32(0, i), :].astype(F32)
                + landed[half, 1, t, rows32(0, i), :].astype(F32)
            )
            if delta:
                tsum[half, t, rows32(half_row, i), :] = total.astype(BF16)
            else:
                own[half, rows32(half_row, i), :] = total

        blocks(n, body)
        for j in {0: (), 1: (2,), 2: (0, 1), 3: (4,)}[delta]:
            message2(g, half, j, t).start()

    def relay2(g, half):
        here = ring(half, 1)[0]
        wait2(g, half, 0)
        for way, onward, step in ((0, 3, 1), (1, 5, 3)):
            target = at(here, step)
            _, half_row, quarter_row, n = rows_of(g, half, way)

            def body(i):
                total = tsum[half, target, rows32(half_row, i), :].astype(F32) + rel2[
                    half, way, rows32(quarter_row, i), :
                ].astype(F32)
                tsum[half, target, rows32(half_row, i), :] = total.astype(BF16)

            blocks(n, body)
            message2(g, half, onward, target).start()

    def finish(g, half):
        wait2(g, half, 1)
        hall_row, half_row, _, n = rows_of(g, half, 0, 2)

        def body(i):
            rows = rows32(half_row, i)
            total = (
                own[half, rows, :]
                + in2[half, 0, rows, :].astype(F32)
                + in2[half, 1, rows, :].astype(F32)
            )
            row = hall_row + i
            position = row // 128
            chip = (x + position + position // 2 - 2 * (position // 3)) % SIDE
            out_ref[rows32(chip * 128, row % 128), :] = total.astype(BF16)

        blocks(n, body)

    def compute(g, order, segments, bounds, services):
        r0, rows = GROUPS[g]

        def product(_, carry):
            deltas_y, deltas_z = carry
            yt, zt = at(y, deltas_y % SIDE), at(z, deltas_z % SIDE)
            column = pl.multiple_of((zt * SIDE + yt) * TILE, TILE)
            acc = jnp.dot(
                hall[pl.ds(r0, rows), :], virt[:, pl.ds(column, TILE)], preferred_element_type=F32
            )
            part[zt, yt, pl.ds(r0, rows), :] = acc.astype(BF16)
            return deltas_y // SIDE, deltas_z // SIDE

        def segment(s, carry):
            low, high = bounds(s)
            after = lax.fori_loop(low, high, product, carry)
            services(s)
            return after

        packed = [
            jnp.int32(sum(pair[k] << (2 * i) for i, pair in enumerate(order))) for k in range(2)
        ]
        lax.fori_loop(0, segments, segment, tuple(packed))

    def both(function, *rest):
        for half in range(2):
            function(*rest[:1], half, *rest[1:])

    def loop(n, function):
        lax.fori_loop(0, n, function, 0)

    def scoped(name, function):
        def run():
            with jax.named_scope(name):
                function()

        return run

    def when(condition, name, function):
        pl.when(condition)(scoped(name, function))

    with jax.named_scope("t_near0"):
        forward_near(0, 0)
    with jax.named_scope("t_part0"):
        all_arrived(0, 0)
    with jax.named_scope("t_virt"):
        virt_copy(2).wait()

    def starts(half, *messages):
        here = ring(half, 0)[0]

        def run():
            for j in messages:
                bulk(half, j, at(here, (2, 2, 1, 1, 3, 3)[j])).start()

        return run

    def services0(s):
        when(
            s == 0,
            "t_s0",
            lambda: (
                starts(1, 0, 1)(),
                [virt_copy(delta).wait() for delta in (1, 3, 0)],
                forward_near(1, 0),
                forward_near(2, 0),
            ),
        )
        when(s == 1, "t_s1", lambda: (starts(0, 0, 1)(), forward_near(3, 0)))
        when(s == 2, "t_s2", lambda: (starts(1, 2)(), loop(1, forward_far)))
        when(s == 3, "t_s3", lambda: (starts(1, 4)(), forward_far(1, 0), forward_far(2, 0)))
        when(s == 4, "t_s4", starts(0, 2, 4))

    with jax.named_scope("t_C0"):
        compute(0, ORDER0, 5, lambda s: (jnp.where(s == 0, 0, 1 + 3 * s), 4 + 3 * s), services0)
    with jax.named_scope("t_far23"):
        forward_far(3, 0)
    with jax.named_scope("t_relay0"):
        relay0(0)
        relay0(1)
    with jax.named_scope("t_part1"):
        all_arrived(3, 2)
        all_arrived(4, 1)
        all_arrived(6, 3)

    def middle0():
        for half in range(2):
            wait0(half, 1)
            for delta in (2, 1, 3, 0):
                middle(0, half, delta)

    def relays(*deltas):
        for delta in deltas:
            for half in range(2):
                relay1(half, delta)

    def bounds1(s):
        return jnp.where(s < 2, s, 2 * s - 2), jnp.where(s < 2, s + 1, 2 * s)

    then1 = {
        3: lambda: relays(2),
        5: lambda: relays(1, 3),
        6: lambda: both(middle, 1, 2),
        8: middle0,
    }

    def services1(s):
        def run(k):
            def go():
                for i in (k,) if k < 2 else (2 * k - 2, 2 * k - 1):
                    send_chunk(*ORDER1[i])
                if k in then1:
                    with jax.named_scope(f"t_then{k}"):
                        then1[k]()

            return go

        @pl.when(s < 4)
        def _():
            for k in range(4):
                when(s == k, f"t_s1{k}", run(k))

        @pl.when(s >= 4)
        def _():
            for k in range(4, 9):
                when(s == k, f"t_s1{k}", run(k))

    with jax.named_scope("t_C1"):
        compute(1, ORDER1, 9, bounds1, services1)
    with jax.named_scope("t_mid13"):
        both(middle, 1, 1)
        both(middle, 1, 3)
    with jax.named_scope("t_rel0"):
        relays(0)
    with jax.named_scope("t_relay21"):
        both(relay2, 1)
    with jax.named_scope("t_relay20"):
        both(relay2, 0)
    with jax.named_scope("t_midown"):
        both(middle, 1, 0)
    with jax.named_scope("t_fin1"):
        both(finish, 1)
    with jax.named_scope("t_fin0"):
        both(finish, 0)
    with jax.named_scope("t_out"):
        out_copy = pltpu.make_async_copy(out_ref, out_hbm, isem.at[0])
        out_copy.start()
        out_copy.wait()

    with jax.named_scope("t_sends"):
        for j, ref in enumerate(
            (halo, hall.at[pl.ds(0, 448)], part.at[pl.ds(0, 3)], part.at[0, pl.ds(0, 3)])
        ):
            remote(ref, ref, sends.at[j], hr.at[0], partner).wait_send()


def local(v_blocks, pair_map, pair_count, occ_coef, virt_coef):
    anywhere = pl.BlockSpec(memory_space=pl.ANY)
    groups = len(GROUPS)
    rows_first = pl.pallas_call(
        kernel,
        out_shape=jax.ShapeDtypeStruct((512, TILE), BF16),
        in_specs=[pl.BlockSpec(memory_space=pltpu.HBM)] * 5,
        out_specs=anywhere,
        scratch_shapes=[
            pltpu.VMEM((512, TILE), BF16),
            pltpu.SMEM((1, 2, PAIR_CAP), jnp.int32),
            pltpu.SMEM((1, 1), jnp.int32),
            pltpu.VMEM((Q, PAIR_CAP, BB, BB), BF16),
            pltpu.VMEM((ROWS, COLS), BF16),
            pltpu.VMEM((NOCC, ROWS), BF16),
            pltpu.VMEM((2, NOCC, NEAR * BB), BF16),
            pltpu.VMEM((HERE + 2 * NEAR, NOCC, BB), F32),
            pltpu.VMEM((BB, PAIR_CAP * BB), BF16),
            pltpu.VMEM((512, ROWS), BF16),
            pltpu.VMEM((SIDE, SIDE, 512, TILE), BF16),
            pltpu.VMEM((2, 2, SIDE, 32, TILE), BF16),
            pltpu.VMEM((2, 2, SIDE, 64, TILE), BF16),
            pltpu.VMEM((2, 2, SIDE, 288, TILE), BF16),
            pltpu.VMEM((2, SIDE, 256, TILE), BF16),
            pltpu.VMEM((2, 256, TILE), F32),
            pltpu.VMEM((2, 2, 128, TILE), BF16),
            pltpu.VMEM((2, 2, 256, TILE), BF16),
            pltpu.SemaphoreType.DMA((3,)),
            pltpu.SemaphoreType.DMA((PIECES,)),
            pltpu.SemaphoreType.DMA((SIDE,)),
            pltpu.SemaphoreType.DMA((4,)),
            pltpu.SemaphoreType.DMA((2,)),
            pltpu.SemaphoreType.DMA((3, PIECES)),
            pltpu.SemaphoreType.DMA((4,)),
            pltpu.SemaphoreType.DMA((2, 2)),
            pltpu.SemaphoreType.DMA((2, 2, SIDE)),
            pltpu.SemaphoreType.DMA((2, groups, 2)),
        ],
        compiler_params=pltpu.CompilerParams(
            collective_id=0, has_side_effects=True, vmem_limit_bytes=44 << 20
        ),
        name="occupied_batch",
    )(jnp.swapaxes(pair_map, 1, 2), pair_count, v_blocks, occ_coef, virt_coef)
    return rows_first.T


def solution(mesh):
    in_specs = (
        P("aux", "basis", None, None),
        P("aux", "basis", None),
        P("aux", "basis"),
        P(None, "basis"),
        P("basis", "aux"),
    )
    out_specs = P(("aux", "basis"), None)
    return jax.shard_map(local, mesh=mesh, in_specs=in_specs, out_specs=out_specs, check_vma=False)
```

```python
import functools

import jax
import jax.numpy as jnp
from jax import lax
from jax.experimental import pallas as pl
from jax.experimental.pallas import tpu as pltpu
from jax.sharding import PartitionSpec as P

BB = 128
NOCC = 8
NEAR = 8
PAIR_CAP = 48
NB = 240
Q = 8
HERE = 15
ROWS = HERE * BB
COLS = 4096
TILE = 256
SIDE = 4
PIECES = 4
GROUPS = ((0, 128), (128, 384))
ORDER0 = (
    (2, 2), (1, 2), (3, 2), (0, 2), (2, 1), (2, 3), (2, 0), (1, 1),
    (3, 1), (0, 1), (1, 3), (3, 3), (0, 3), (1, 0), (3, 0), (0, 0),
)
ORDER1 = (
    (2, 2), (1, 2), (2, 1), (3, 2), (2, 3), (1, 1), (3, 3), (1, 3),
    (3, 1), (0, 2), (2, 0), (0, 1), (1, 0), (0, 3), (3, 0), (0, 0),
)
MESH = pl.DeviceIdType.MESH
F32 = jnp.float32
BF16 = jnp.bfloat16


def kernel(
    pm_hbm,
    pc_hbm,
    v_hbm,
    occ_hbm,
    virt_hbm,
    out_hbm,
    out_ref,
    pm,
    pc,
    v,
    virt,
    occ,
    halo,
    tab,
    lhs,
    hall,
    part,
    rel0,
    in0,
    in1,
    tsum,
    own,
    rel2,
    in2,
    isem,
    vsem,
    wsem,
    sends,
    hr,
    gr,
    gr_all,
    m0,
    m1,
    m2,
):
    aux = lax.axis_index("aux")
    basis = lax.axis_index("basis")
    x, c = aux // 2, aux % 2
    z, y = basis // SIDE, basis % SIDE

    partner = (2 * x + 1 - c, basis)
    x_up = (2 * ((x + 1) % SIDE) + c, basis)
    x_down = (2 * ((x + 3) % SIDE) + c, basis)
    y_up = (aux, z * SIDE + (y + 1) % SIDE)
    y_down = (aux, z * SIDE + (y + 3) % SIDE)
    z_up = (aux, ((z + 1) % SIDE) * SIDE + y)
    z_down = (aux, ((z + 3) % SIDE) * SIDE + y)
    b_up = (aux, (basis + 1) % (SIDE * SIDE))
    b_down = (aux, (basis + SIDE * SIDE - 1) % (SIDE * SIDE))
    x_relay = (2 * ((x + 1 + 2 * c) % SIDE) + c, basis)

    barrier = pltpu.get_barrier_semaphore()
    peers = (b_up, b_down, z_up, z_down, y_up, y_down, x_up, x_down, partner)
    for peer in peers:
        pl.semaphore_signal(
            barrier, inc=1, device_id={"aux": peer[0], "basis": peer[1]}, device_id_type=MESH
        )

    def remote(src, dst, send, recv, peer):
        return pltpu.make_async_remote_copy(
            src_ref=src,
            dst_ref=dst,
            send_sem=send,
            recv_sem=recv,
            device_id={"aux": peer[0], "basis": peer[1]},
            device_id_type=MESH,
        )

    small = (
        pltpu.make_async_copy(occ_hbm, occ, isem.at[0]),
        pltpu.make_async_copy(pm_hbm, pm, isem.at[1]),
        pltpu.make_async_copy(pc_hbm, pc, isem.at[2]),
    )
    for copy in small:
        copy.start()

    def v_copy(p):
        return pltpu.make_async_copy(v_hbm.at[pl.ds(2 * p, 2)], v.at[pl.ds(2 * p, 2)], vsem.at[p])

    def virt_copy(delta):
        columns = pl.ds(pl.multiple_of((z + delta) % SIDE * 1024, 1024), 1024)
        return pltpu.make_async_copy(
            virt_hbm.at[:, columns], virt.at[:, columns], wsem.at[delta]
        )

    for p in range(PIECES):
        v_copy(p).start()
    with jax.named_scope("t_barrier"):
        pl.semaphore_wait(barrier, len(peers))

    width = NEAR * BB
    with jax.named_scope("t_occ"):
        small[0].wait()
    to_up = remote(occ.at[:, pl.ds(ROWS - width, width)], halo.at[0], sends.at[0], hr.at[0], b_up)
    to_down = remote(occ.at[:, pl.ds(0, width)], halo.at[1], sends.at[0], hr.at[1], b_down)
    to_up.start()
    to_down.start()
    for j in range(HERE):
        tab[NEAR + j] = occ[:, j * BB : (j + 1) * BB].astype(F32)
    with jax.named_scope("t_halo"):
        to_up.wait_recv()
        to_down.wait_recv()
    with jax.named_scope("t_small"):
        small[1].wait()
        small[2].wait()
    for delta in (2, 1, 3, 0):
        virt_copy(delta).start()
    for j in range(NEAR):
        tab[j] = halo[0, :, j * BB : (j + 1) * BB].astype(F32)
        tab[NEAR + HERE + j] = halo[1, :, j * BB : (j + 1) * BB].astype(F32)

    first = basis * HERE
    row_block = lax.broadcasted_iota(jnp.int32, (BB, BB), 0) // NOCC

    def build(k, _):
        mu = pm[0, 0, k]
        nu = pm[0, 1, k]
        place = jnp.where(k < pc[0, 0], mu - first, -1)
        pos = jnp.clip(lax.rem(nu - first + NEAR + NB, NB), 0, HERE + 2 * NEAR - 1)
        stack = jnp.concatenate([tab[pos]] * (BB // NOCC), axis=0)
        lhs[:, pl.ds(pl.multiple_of(k * BB, BB), BB)] = jnp.where(
            row_block == place, stack, 0.0
        ).astype(BF16)
        return 0

    with jax.named_scope("t_build"):
        lax.fori_loop(0, PAIR_CAP, build, 0, unroll=4)

    def piece_ref(position, core, p):
        return hall.at[pl.ds(pl.multiple_of(position * 128 + core * 64 + p * 16, 16), 16)]

    def gather_sem(message, p):
        if message in (1, 2, 5):
            return gr.at[(1, 2, 5).index(message), p]
        return gr_all.at[(0, 3, 4, 6).index(message)]

    def gather(message, p, position_src, position_dst, core, peer):
        return remote(
            piece_ref(position_src, core, p),
            piece_ref(position_dst, core, p),
            sends.at[1],
            gather_sem(message, p),
            peer,
        )

    def arrived(message, p, position, core, peer):
        ref = piece_ref(position, core, p)
        remote(ref, ref, sends.at[1], gather_sem(message, p), peer).wait_recv()

    def all_arrived(message, position):
        ref = hall.at[pl.ds(pl.multiple_of(position * 128 + (1 - c) * 64, 64), 64)]
        remote(ref, ref, sends.at[1], gather_sem(message, 0), partner).wait_recv()

    def first_half(p, _):
        v_copy(p).wait()
        acc = jnp.zeros((BB, 2 * BB), F32)
        for k in range(0, PAIR_CAP, 2):
            w = jnp.concatenate(
                [
                    jnp.concatenate([v[2 * p + e, k], v[2 * p + e, k + 1]], axis=1)
                    for e in range(2)
                ],
                axis=0,
            )
            acc += lax.dot_general(
                lhs[:, k * BB : (k + 2) * BB],
                w,
                (((1,), (1,)), ((), ())),
                preferred_element_type=F32,
            )
        row = pl.multiple_of(c * 64 + p * 16, 16)
        for j in range(HERE):
            lines = acc[j * NOCC : (j + 1) * NOCC]
            both = jnp.concatenate([lines[:, :BB], lines[:, BB:]], axis=0)
            hall[pl.ds(row, 16), j * BB : (j + 1) * BB] = both.astype(BF16)
        gather(0, p, 0, 0, c, partner).start()
        gather(1, p, 0, 2, c, x_up).start()
        gather(2, p, 0, 1, c, x_down).start()
        return 0

    with jax.named_scope("t_first"):
        lax.fori_loop(0, PIECES, first_half, 0)

    def forward_near(p, _):
        arrived(1, p, 2, c, x_down)
        gather(3, p, 2, 2, c, partner).start()
        arrived(2, p, 1, c, x_up)
        gather(4, p, 1, 1, c, partner).start()
        gather(5, p, 2 - c, 3, c, x_relay).start()
        return 0

    def forward_far(p, _):
        arrived(5, p, 3, c, x_relay)
        gather(6, p, 3, 3, c, partner).start()
        return 0

    def rows_of(g, half, which, count=1):
        r0, rows = GROUPS[g]
        quarter = rows // 4
        return (
            r0 + half * 2 * quarter + which * quarter,
            r0 // 2 + which * quarter,
            r0 // 4,
            quarter * count,
        )

    def ring(half, phase):
        return (y, y_up, y_down) if half == phase else (z, z_up, z_down)

    def at(here, delta):
        return (here + delta) % SIDE

    KINDS = ((0, 0, 0), (1, 1, 0), (1, 0, 1), (0, 0, 1), (0, 1, 1), (1, 1, 1))

    def bulk(half, j, target):
        which, way, landing = KINDS[j]
        hall_row, half_row, quarter_row, n = rows_of(0, half, which)
        rows = pl.ds(hall_row, n)
        return remote(
            part.at[:, target, rows] if half == 0 else part.at[target, :, rows],
            in0.at[half, way, :, pl.ds(half_row, n)] if landing else rel0.at[half, way],
            sends.at[2],
            m0.at[landing, half],
            ring(half, 0)[1 + way],
        )

    R0, RN = GROUPS[1]
    QUARTER = RN // 4

    def single(half, which, way, landing, target, t):
        put = which * QUARTER if landing else 2 * QUARTER
        zt, yt = (t, target) if half == 0 else (target, t)
        return remote(
            part.at[zt, yt, pl.ds(R0 + (2 * half + which) * QUARTER, QUARTER)],
            in1.at[half, way, t, pl.ds(put, QUARTER)],
            sends.at[2],
            m1.at[landing, half, t],
            ring(half, 0)[1 + way],
        )

    def send_chunk(dy, dz):
        yt, zt = at(y, dy), at(z, dz)
        for half, d, target, t in ((0, dy, yt, zt), (1, dz, zt, yt)):
            if d == 2:
                single(half, 0, 0, 0, target, t).start()
                single(half, 1, 1, 0, target, t).start()
            elif d:
                single(half, 1 - d // 2, d // 2, 1, target, t).start()

    def message2(g, half, j, target):
        which, way, landing = KINDS[j]
        _, half_row, quarter_row, n = rows_of(g, half, which)
        if landing:
            dst = in2.at[half, way, pl.ds(half_row, n)]
        else:
            dst = rel2.at[half, way, pl.ds(quarter_row, n)]
        return remote(
            tsum.at[half, target, pl.ds(half_row, n)],
            dst,
            sends.at[3],
            m2.at[landing, g, half],
            ring(half, 1)[1 + way],
        )

    def wait1(half, t, landing):
        rows = pl.ds(0, 2 * QUARTER) if landing else pl.ds(2 * QUARTER, QUARTER)
        ref = in1.at[half, :, t, rows]
        remote(ref, ref, sends.at[2], m1.at[landing, half, t], ring(half, 0)[1]).wait_recv()

    def wait0(half, landing):
        ref = in0.at[half] if landing else rel0.at[half]
        remote(ref, ref, sends.at[2], m0.at[landing, half], ring(half, 0)[1]).wait_recv()

    def wait2(g, half, landing):
        _, half_row, quarter_row, n = rows_of(g, half, 0)
        if landing:
            ref = in2.at[half, :, pl.ds(half_row, 2 * n)]
        else:
            ref = rel2.at[half, :, pl.ds(quarter_row, n)]
        remote(ref, ref, sends.at[3], m2.at[landing, g, half], ring(half, 1)[1]).wait_recv()

    def rows_by(size, start, i):
        return pl.ds(pl.multiple_of(start + i, 32), size)

    def blocks(n, body, size=32):
        def step(i, _):
            body(i * size)
            return 0

        lax.fori_loop(0, n // size, step, 0)

    def rows32(start, i):
        return pl.ds(pl.multiple_of(start + i, 32), 32)

    def relay1(half, delta):
        here = ring(half, 0)[0]
        t = at(z if half == 0 else y, delta)
        wait1(half, t, 0)
        for way, step in ((0, 1), (1, 3)):
            target = at(here, step)
            zt, yt = (t, target) if half == 0 else (target, t)
            row = R0 + (2 * half + way) * QUARTER

            def body(i):
                total = part[zt, yt, rows_by(QUARTER, row, i), :].astype(F32) + in1[
                    half, way, t, rows_by(QUARTER, 2 * QUARTER, i), :
                ].astype(F32)
                part[zt, yt, rows_by(QUARTER, row, i), :] = total.astype(BF16)

            blocks(QUARTER, body, QUARTER)
            single(half, way, way, 1, target, t).start()

    def relay0(half):
        here = ring(half, 0)[0]
        wait0(half, 0)
        for way, onward, step in ((0, 3, 1), (1, 5, 3)):
            target = at(here, step)
            row, _, _, n = rows_of(0, half, way)

            def body(t, _):
                zt, yt = (t, target) if half == 0 else (target, t)
                total = part[zt, yt, pl.ds(row, n), :].astype(F32) + rel0[half, way, t].astype(F32)
                part[zt, yt, pl.ds(row, n), :] = total.astype(BF16)
                return 0

            lax.fori_loop(0, SIDE, body, 0)
            bulk(half, onward, target).start()

    def middle(g, half, delta):
        t = at(z if half == 0 else y, delta)
        if g:
            wait1(half, t, 1)
        zt, yt = (t, y) if half == 0 else (z, t)
        hall_row, half_row, _, n = rows_of(g, half, 0, 2)
        landed = in1 if g else in0

        def body(i):
            total = (
                part[zt, yt, rows_by(GROUPS[g][1] // 4, hall_row, i), :].astype(F32)
                + landed[half, 0, t, rows_by(GROUPS[g][1] // 4, 0, i), :].astype(F32)
                + landed[half, 1, t, rows_by(GROUPS[g][1] // 4, 0, i), :].astype(F32)
            )
            if delta:
                tsum[half, t, rows_by(GROUPS[g][1] // 4, half_row, i), :] = total.astype(BF16)
            else:
                own[half, rows_by(GROUPS[g][1] // 4, half_row, i), :] = total

        blocks(n, body, GROUPS[g][1] // 4)
        for j in {0: (), 1: (2,), 2: (0, 1), 3: (4,)}[delta]:
            message2(g, half, j, t).start()

    def relay2(g, half):
        here = ring(half, 1)[0]
        wait2(g, half, 0)
        for way, onward, step in ((0, 3, 1), (1, 5, 3)):
            target = at(here, step)
            _, half_row, quarter_row, n = rows_of(g, half, way)

            def body(i):
                total = tsum[half, target, rows_by(GROUPS[g][1] // 4, half_row, i), :].astype(F32) + rel2[
                    half, way, rows_by(GROUPS[g][1] // 4, quarter_row, i), :
                ].astype(F32)
                tsum[half, target, rows_by(GROUPS[g][1] // 4, half_row, i), :] = total.astype(BF16)

            blocks(n, body, GROUPS[g][1] // 4)
            message2(g, half, onward, target).start()

    def finish(g, half):
        wait2(g, half, 1)
        hall_row, half_row, _, n = rows_of(g, half, 0, 2)

        def body(i):
            rows = rows32(half_row, i)
            total = (
                own[half, rows, :]
                + in2[half, 0, rows, :].astype(F32)
                + in2[half, 1, rows, :].astype(F32)
            )
            row = hall_row + i
            position = row // 128
            chip = (x + position + position // 2 - 2 * (position // 3)) % SIDE
            out_ref[rows32(chip * 128, row % 128), :] = total.astype(BF16)

        blocks(n, body)

    def compute(g, order, segments, bounds, services):
        r0, rows = GROUPS[g]

        def product(_, carry):
            deltas_y, deltas_z = carry
            yt, zt = at(y, deltas_y % SIDE), at(z, deltas_z % SIDE)
            column = pl.multiple_of((zt * SIDE + yt) * TILE, TILE)
            acc = jnp.dot(
                hall[pl.ds(r0, rows), :], virt[:, pl.ds(column, TILE)], preferred_element_type=F32
            )
            part[zt, yt, pl.ds(r0, rows), :] = acc.astype(BF16)
            return deltas_y // SIDE, deltas_z // SIDE

        def segment(s, carry):
            low, high = bounds(s)
            after = lax.fori_loop(low, high, product, carry)
            services(s)
            return after

        packed = [
            jnp.int32(sum(pair[k] << (2 * i) for i, pair in enumerate(order))) for k in range(2)
        ]
        lax.fori_loop(0, segments, segment, tuple(packed))

    def both(function, *rest):
        for half in range(2):
            function(*rest[:1], half, *rest[1:])

    def loop(n, function):
        lax.fori_loop(0, n, function, 0)

    def scoped(name, function):
        def run():
            with jax.named_scope(name):
                function()

        return run

    def when(condition, name, function):
        pl.when(condition)(scoped(name, function))

    with jax.named_scope("t_near0"):
        forward_near(0, 0)
    with jax.named_scope("t_part0"):
        all_arrived(0, 0)
    with jax.named_scope("t_virt"):
        virt_copy(2).wait()

    def starts(half, *messages):
        here = ring(half, 0)[0]

        def run():
            for j in messages:
                bulk(half, j, at(here, (2, 2, 1, 1, 3, 3)[j])).start()

        return run

    def services0(s):
        when(
            s == 0,
            "t_s0",
            lambda: (
                starts(1, 0, 1)(),
                [virt_copy(delta).wait() for delta in (1, 3, 0)],
                forward_near(1, 0),
                forward_near(2, 0),
            ),
        )
        when(s == 1, "t_s1", lambda: (starts(0, 0, 1)(), forward_near(3, 0)))
        when(s == 2, "t_s2", lambda: (starts(1, 2)(), loop(1, forward_far)))
        when(s == 3, "t_s3", lambda: (starts(1, 4)(), forward_far(1, 0), forward_far(2, 0)))
        when(s == 4, "t_s4", starts(0, 2, 4))

    with jax.named_scope("t_C0"):
        compute(0, ORDER0, 5, lambda s: (jnp.where(s == 0, 0, 1 + 3 * s), 4 + 3 * s), services0)
    with jax.named_scope("t_far23"):
        forward_far(3, 0)
    with jax.named_scope("t_relay0"):
        relay0(0)
        relay0(1)
    with jax.named_scope("t_part1"):
        all_arrived(3, 2)
        all_arrived(4, 1)
        all_arrived(6, 3)

    def middle0():
        for half in range(2):
            wait0(half, 1)
            for delta in (2, 1, 3, 0):
                middle(0, half, delta)

    def relays(*deltas):
        for delta in deltas:
            for half in range(2):
                relay1(half, delta)

    def bounds1(s):
        return jnp.where(s < 2, s, 2 * s - 2), jnp.where(s < 2, s + 1, 2 * s)

    then1 = {
        3: lambda: relays(2),
        5: lambda: relays(1, 3),
        6: lambda: both(middle, 1, 2),
        8: middle0,
    }

    def services1(s):
        def run(k):
            def go():
                for i in (k,) if k < 2 else (2 * k - 2, 2 * k - 1):
                    send_chunk(*ORDER1[i])
                if k in then1:
                    with jax.named_scope(f"t_then{k}"):
                        then1[k]()

            return go

        @pl.when(s < 4)
        def _():
            for k in range(4):
                when(s == k, f"t_s1{k}", run(k))

        @pl.when(s >= 4)
        def _():
            for k in range(4, 9):
                when(s == k, f"t_s1{k}", run(k))

    with jax.named_scope("t_C1"):
        compute(1, ORDER1, 9, bounds1, services1)
    with jax.named_scope("t_mid13"):
        both(middle, 1, 1)
        both(middle, 1, 3)
    with jax.named_scope("t_rel0"):
        relays(0)
    with jax.named_scope("t_relay21"):
        both(relay2, 1)
    with jax.named_scope("t_relay20"):
        both(relay2, 0)
    with jax.named_scope("t_midown"):
        both(middle, 1, 0)
    with jax.named_scope("t_fin1"):
        both(finish, 1)
    with jax.named_scope("t_fin0"):
        both(finish, 0)
    with jax.named_scope("t_out"):
        out_copy = pltpu.make_async_copy(out_ref, out_hbm, isem.at[0])
        out_copy.start()
        out_copy.wait()

    with jax.named_scope("t_sends"):
        for j, ref in enumerate(
            (halo, hall.at[pl.ds(0, 448)], part.at[pl.ds(0, 3)], part.at[0, pl.ds(0, 3)])
        ):
            remote(ref, ref, sends.at[j], hr.at[0], partner).wait_send()


def local(v_blocks, pair_map, pair_count, occ_coef, virt_coef):
    anywhere = pl.BlockSpec(memory_space=pl.ANY)
    groups = len(GROUPS)
    rows_first = pl.pallas_call(
        kernel,
        out_shape=jax.ShapeDtypeStruct((512, TILE), BF16),
        in_specs=[pl.BlockSpec(memory_space=pltpu.HBM)] * 5,
        out_specs=anywhere,
        scratch_shapes=[
            pltpu.VMEM((512, TILE), BF16),
            pltpu.SMEM((1, 2, PAIR_CAP), jnp.int32),
            pltpu.SMEM((1, 1), jnp.int32),
            pltpu.VMEM((Q, PAIR_CAP, BB, BB), BF16),
            pltpu.VMEM((ROWS, COLS), BF16),
            pltpu.VMEM((NOCC, ROWS), BF16),
            pltpu.VMEM((2, NOCC, NEAR * BB), BF16),
            pltpu.VMEM((HERE + 2 * NEAR, NOCC, BB), F32),
            pltpu.VMEM((BB, PAIR_CAP * BB), BF16),
            pltpu.VMEM((512, ROWS), BF16),
            pltpu.VMEM((SIDE, SIDE, 512, TILE), BF16),
            pltpu.VMEM((2, 2, SIDE, 32, TILE), BF16),
            pltpu.VMEM((2, 2, SIDE, 64, TILE), BF16),
            pltpu.VMEM((2, 2, SIDE, 288, TILE), BF16),
            pltpu.VMEM((2, SIDE, 256, TILE), BF16),
            pltpu.VMEM((2, 256, TILE), F32),
            pltpu.VMEM((2, 2, 128, TILE), BF16),
            pltpu.VMEM((2, 2, 256, TILE), BF16),
            pltpu.SemaphoreType.DMA((3,)),
            pltpu.SemaphoreType.DMA((PIECES,)),
            pltpu.SemaphoreType.DMA((SIDE,)),
            pltpu.SemaphoreType.DMA((4,)),
            pltpu.SemaphoreType.DMA((2,)),
            pltpu.SemaphoreType.DMA((3, PIECES)),
            pltpu.SemaphoreType.DMA((4,)),
            pltpu.SemaphoreType.DMA((2, 2)),
            pltpu.SemaphoreType.DMA((2, 2, SIDE)),
            pltpu.SemaphoreType.DMA((2, groups, 2)),
        ],
        compiler_params=pltpu.CompilerParams(
            collective_id=0, has_side_effects=True, vmem_limit_bytes=44 << 20
        ),
        name="occupied_batch",
    )(jnp.swapaxes(pair_map, 1, 2), pair_count, v_blocks, occ_coef, virt_coef)
    return rows_first.T


def solution(mesh):
    in_specs = (
        P("aux", "basis", None, None),
        P("aux", "basis", None),
        P("aux", "basis"),
        P(None, "basis"),
        P("basis", "aux"),
    )
    out_specs = P(("aux", "basis"), None)
    return jax.shard_map(local, mesh=mesh, in_specs=in_specs, out_specs=out_specs, check_vma=False)
```
